256 devices in a mesh: grp: 16 (over y, z_hi, core), dev: 16 (over z_lo, x).
Axes of the slice: x: 4, y: 4, z: 8 (z_hi: 2, z_lo: 4; z = z_hi * 4 + z_lo), core: 2. Of those that a mesh axis runs over, the one named last changes fastest.
Arguments:
- panels: bfloat16 [256, 1536, 512], P(('grp', 'dev')), may hold values from -0.19921875 to 0.19921875
- panel_owner: int32 [16, 3], replicated, may hold values from 0 to 15, as said below
- interface_cols: bfloat16 [1536, 65536], P(None, ('grp', 'dev')), may hold values from -6 to 6
- border: bfloat16 [16384, 1536], P('grp', 'dev'), may hold values from -0.15625 to 0.15625
- block_rows: int32 [16, 8], replicated, may hold values from 0 to 31, as said below
- pattern: int32 [32, 32], P('grp', 'dev'), may hold values 0 or 1
- block_x: bfloat16 [4096, 256], P('dev'), may hold values from -0.09375 to 0.09375
Outputs:
- schur: bfloat16 [4096, 4096], P('grp', 'dev')
- product: float32 [4096, 256], P('grp')
The draws below stay inside these ranges and needn't reach their ends.
Inputs may be any that keep to these rules, and one draw needn't show every extreme that they name: `panel_owner`: in each row the values are distinct. `block_rows`: in each row the values are distinct; for each subdomain the block rows with the same value of block // 2 (their owner group) come exactly 2 at a time; in every draw some owner group receives 2 block rows from every subdomain.
All inputs are finite; a program needn't handle non-finite values. No bound on the sum of `pattern` on one device may be relied on, other than what follows from the above.
Results may differ from the reference program's by a relative error of at most 0.017.
Values may be sent and summed in bfloat16 or wider, within the bound.
No kernel may reach another device: no remote copies, remote signals or barrier semaphores. Data moves between devices by JAX's collectives and lax.ppermute only.
A program may use at most 64 MiB of HBM per device.

```python
import jax
import jax.numpy as jnp
from jax import lax

N = 1536
PW = 512
BR = 1024
RB = 128
XC = 256
CAP = 2
GROUPS = 16
DEVS = 16
NPAN = 3
BLK_GRP = 8
NSEL = 4
M = 4096
MB = 32
BPO = 2
GCOLS = 65536
N_GRP = 16
N_DEV = 16


def draw_panel_owner(key, part):
    keys = jax.random.split(jax.random.fold_in(key, 11), GROUPS)
    perms = jax.vmap(lambda single: jax.random.permutation(single, DEVS))(keys)
    return perms[:, :NPAN].astype(jnp.int32)


def draw_block_rows(key, part):
    base = jax.random.fold_in(key, 23)
    favored = jax.random.randint(jax.random.fold_in(base, 1), (), 0, GROUPS)
    keys = jax.random.split(jax.random.fold_in(base, 2), GROUPS)

    def one_group(single):
        first, second, third = jax.random.split(single, 3)
        scores = jax.random.randint(first, (GROUPS,), 0, GROUPS)
        scores = scores + jnp.where(jnp.arange(GROUPS) == favored, 2 * GROUPS, 0)
        distinct = scores * GROUPS + jnp.arange(GROUPS)
        chosen = jnp.argsort(-distinct, stable=True)[:NSEL]
        inner_keys = jax.random.split(second, NSEL)
        locals_ = jax.vmap(lambda sub: jax.random.permutation(sub, BPO)[:CAP])(inner_keys)
        blocks = (chosen[:, None] * BPO + locals_).reshape(-1)
        order = jax.random.permutation(third, BLK_GRP)
        return blocks[order]
    return jax.vmap(one_group)(keys).astype(jnp.int32)


def touch_ends(entries, key, smallest, largest):
    shape = entries.shape
    spot = [jax.random.randint(jax.random.fold_in(key, axis), (), 0, shape[axis]) for axis in range(len(shape))]
    entries = entries.at[tuple(spot)].set(smallest)
    longest = shape.index(max(shape))
    spot[longest] = (spot[longest] + 1) % shape[longest]
    return entries.at[tuple(spot)].set(largest)


def shard_levels(own_key, shape, cuts, low, high):
    level = 1.0
    for dim, parts in cuts:
        heights = jax.random.uniform(jax.random.fold_in(jax.random.fold_in(own_key, 6), dim), (parts,), jnp.float32, low / len(cuts), high / len(cuts))
        level = level * jnp.repeat(jnp.exp(heights), shape[dim] // parts).reshape((-1,) + (1,) * (len(shape) - 1 - dim))
    return level


def normal_values(rng, dims, width, most, shards=(), kind=jnp.bfloat16):
    gain = shard_levels(rng, dims, shards, -0.22, 0.18) if shards else 1.0
    entries = jax.random.normal(rng, dims, jnp.float32) * width * gain
    return jnp.minimum(jnp.maximum(entries, -most), most).astype(kind)


def setup_inputs(seed: int = 0) -> dict:
    arg_keys = jax.random.split(jax.random.key(seed), 8)
    return {
        "panels": normal_values(arg_keys[0], (N_GRP * N_DEV, N, PW), 0.03, 0.19921875, ((0, 256),)),
        "panel_owner": draw_panel_owner(jax.random.fold_in(arg_keys[7], 71), 0),
        "interface_cols": normal_values(arg_keys[2], (N, GCOLS), 1.0, 6.0, ((1, 256),)),
        "border": normal_values(arg_keys[3], (N_GRP * BR, N), N ** -0.5, 0.15625, ((0, 16), (1, 16))),
        "block_rows": draw_block_rows(jax.random.fold_in(arg_keys[7], 71), 0),
        "pattern": touch_ends((jax.random.randint(arg_keys[5], (MB, MB), 0, 4) < 3).astype(jnp.int32), jax.random.fold_in(arg_keys[5], 1), 0, 1),
        "block_x": normal_values(arg_keys[6], (M, XC), M ** -0.5, 0.09375, ((0, 16),)),
    }


def solve_group(slots, owners, columns):
    lower = lax.broadcasted_iota(jnp.int32, (PW, PW), 0) > lax.broadcasted_iota(jnp.int32, (PW, PW), 1)
    unit = jnp.eye(PW, dtype=jnp.bfloat16)
    remain = [columns[step * PW:(step + 1) * PW].astype(jnp.float32) for step in range(NPAN)]
    solved = []
    for step in range(NPAN):
        slot = slots[owners[step]]
        diag_block = slot[step * PW:(step + 1) * PW]
        inverse = jnp.where(lower, diag_block, jnp.zeros((), jnp.bfloat16)) + unit
        current = jnp.dot(inverse, remain[step].astype(jnp.bfloat16), preferred_element_type=jnp.float32).astype(jnp.bfloat16)
        solved.append(current)
        if step + 1 < NPAN:
            below = jnp.dot(slot[(step + 1) * PW:], current, preferred_element_type=jnp.float32)
            for later in range(step + 1, NPAN):
                offset = (later - step - 1) * PW
                remain[later] = remain[later] - below[offset:offset + PW]
    return jnp.concatenate(solved, axis=0)


def reference(panels, panel_owner, interface_cols, border, block_rows, pattern, block_x):
    slots_all = panels.reshape(GROUPS, DEVS, N, PW)
    total = jnp.zeros((M, M), jnp.float32)
    inner = jnp.arange(RB, dtype=jnp.int32)
    for group in range(GROUPS):
        answer = solve_group(slots_all[group], panel_owner[group], interface_cols[:, group * M:(group + 1) * M])
        tile = jnp.dot(border[group * BR:(group + 1) * BR], answer, preferred_element_type=jnp.float32)
        targets = (block_rows[group][:, None] * RB + inner[None, :]).reshape(-1).astype(jnp.int32)
        total = total.at[targets].add(tile)
    masked = total.reshape(MB, RB, MB, RB) * pattern.astype(jnp.float32)[:, None, :, None]
    schur = masked.reshape(M, M).astype(jnp.bfloat16)
    product = jnp.dot(schur, block_x, preferred_element_type=jnp.float32)
    return schur, product
```

```python
import functools

import jax
import jax.numpy as jnp
from jax import lax
from jax.experimental import pallas as pl
from jax.experimental.pallas import tpu as pltpu
from jax.sharding import PartitionSpec as P

F32 = jnp.float32
BF16 = jnp.bfloat16
ANY = pl.BlockSpec(memory_space=pl.ANY)
VMEM = pl.BlockSpec(memory_space=pltpu.VMEM)
SMEM = pl.BlockSpec(memory_space=pltpu.SMEM)


def hop_x(value, dx):
    perm = [(z * 4 + x, z * 4 + (x + dx) % 4) for z in range(4) for x in range(4)]
    return lax.ppermute(value, "dev", perm)


def hop_z(value, bits):
    perm = [(z * 4 + x, (z ^ bits) * 4 + x) for z in range(4) for x in range(4)]
    return lax.ppermute(value, "dev", perm)


def hop_y(value, dy):
    perm = [(y * 4 + r, ((y + dy) % 4) * 4 + r) for y in range(4) for r in range(4)]
    return lax.ppermute(value, "grp", perm)


def swap_grp(value, bits):
    return lax.ppermute(value, "grp", [(g, g ^ bits) for g in range(16)])


def gather_blocks(block):
    low = jnp.stack([block, hop_z(block, 1)])
    high = jnp.stack([hop_z(block, 2), hop_z(block, 3)])
    low_left = hop_x(low, 1)
    high_right = hop_x(high, -1)
    high_left = hop_x(high, 1)
    low_right = hop_x(low, -1)
    low_far = hop_x(low_left, 1)
    high_far = hop_x(high_right, -1)
    return [low, high, low_left, high_left, low_right, high_right, low_far, high_far]


def block_sources(dev):
    z, x = dev // 4, dev % 4
    order = []
    for dx in (0, 3, 1, 2):
        for bits in range(4):
            order.append((z ^ bits) * 4 + (x + dx) % 4)
    return jnp.stack(order).astype(jnp.int32)


def solve_kernel(sources, *refs):
    blocks, (cols, out, pan0, pan1, pan2, sem) = refs[:8], refs[8:]
    width = 512
    copies = []
    for part in range(16):
        block = blocks[part // 2].at[part % 2]
        source = sources[part]
        for index, (pan, first, rows) in enumerate(((pan0, 0, 96), (pan1, 96, 64), (pan2, 160, 32))):
            start = pl.multiple_of(source * rows, rows)
            copies.append(
                pltpu.make_async_copy(
                    block.at[pl.ds(first, rows)], pan.at[pl.ds(start, rows)], sem.at[part * 3 + index]
                )
            )
    for copy in copies:
        copy.start()
    for copy in copies:
        copy.wait()
    row = lax.broadcasted_iota(jnp.int32, (width, width), 0)
    col = lax.broadcasted_iota(jnp.int32, (width, width), 1)

    def unit_lower(pan):
        below = jnp.where(row > col, pan[:width].astype(F32), 0.0)
        return jnp.where(row == col, 1.0, below).astype(BF16)

    first = jnp.dot(unit_lower(pan0), cols[:width], preferred_element_type=F32).astype(BF16)
    out[:width] = first
    rest = cols[width:].astype(F32) - jnp.dot(pan0[width:], first, preferred_element_type=F32)
    second = jnp.dot(unit_lower(pan1), rest[:width].astype(BF16), preferred_element_type=F32).astype(BF16)
    out[width : 2 * width] = second
    rest = rest[width:] - jnp.dot(pan1[width:], second, preferred_element_type=F32)
    out[2 * width :] = jnp.dot(unit_lower(pan2), rest.astype(BF16), preferred_element_type=F32).astype(BF16)


def solve(blocks, sources, cols):
    return pl.pallas_call(
        solve_kernel,
        out_shape=jax.ShapeDtypeStruct((1536, 256), BF16),
        in_specs=[SMEM] + [ANY] * 8 + [VMEM],
        out_specs=VMEM,
        scratch_shapes=[
            pltpu.VMEM((1536, 512), BF16),
            pltpu.VMEM((1024, 512), BF16),
            pltpu.VMEM((512, 512), BF16),
            pltpu.SemaphoreType.DMA((48,)),
        ],
        cost_estimate=pl.CostEstimate(flops=800_000_000, bytes_accessed=5_000_000, transcendentals=0),
        compiler_params=pltpu.CompilerParams(vmem_limit_bytes=32 << 20),
        name="solve",
    )(sources, *blocks, cols)


def tile_kernel(sources, *refs):
    blocks, (answer, out, border, sem) = refs[:8], refs[8:]
    copies = []
    for part in range(16):
        start = pl.multiple_of(sources[part] * 96, 96)
        copies.append(
            pltpu.make_async_copy(
                blocks[part // 2].at[part % 2], border.at[pl.ds(start, 96)], sem.at[part]
            )
        )
    for copy in copies:
        copy.start()
    for copy in copies:
        copy.wait()
    for block in range(4):
        part = border[:, block * 256 : (block + 1) * 256]
        tile = lax.dot_general(part, answer[...], (((0,), (0,)), ((), ())), preferred_element_type=F32)
        out[2 * block : 2 * block + 2] = tile.reshape(2, 128, 256).astype(BF16)


def make_tile(blocks, sources, answer):
    return pl.pallas_call(
        tile_kernel,
        out_shape=jax.ShapeDtypeStruct((8, 128, 256), BF16),
        in_specs=[SMEM] + [ANY] * 8 + [VMEM],
        out_specs=VMEM,
        scratch_shapes=[pltpu.VMEM((1536, 1024), BF16), pltpu.SemaphoreType.DMA((16,))],
        cost_estimate=pl.CostEstimate(flops=800_000_000, bytes_accessed=5_000_000, transcendentals=0),
        compiler_params=pltpu.CompilerParams(vmem_limit_bytes=32 << 20),
        name="tile",
    )(sources, *blocks, answer)


def place_kernel(slots, own, other, stay, up1, up2, up3, total):
    total[...] = jnp.zeros_like(total)
    for part in range(16):
        source = own if part < 8 else other
        slot = slots[part]

        @pl.when(slot >= 0)
        def _():
            total[slot] += source[part % 8].astype(F32)

    for index, out in enumerate((stay, up1, up2, up3)):
        out[...] = total[index * 4 : index * 4 + 4].astype(BF16)


def place(slots, own, other):
    return pl.pallas_call(
        place_kernel,
        out_shape=[jax.ShapeDtypeStruct((4, 128, 256), BF16)] * 4,
        in_specs=[SMEM, VMEM, VMEM],
        out_specs=[VMEM] * 4,
        scratch_shapes=[pltpu.VMEM((16, 128, 256), F32)],
        cost_estimate=pl.CostEstimate(flops=1_000_000, bytes_accessed=2_000_000, transcendentals=0),
        compiler_params=pltpu.CompilerParams(vmem_limit_bytes=32 << 20),
        name="place",
    )(slots, own, other)


def local(panels, panel_owner, interface_cols, border, block_rows, pattern, block_x):
    group = lax.axis_index("grp")
    dev = lax.axis_index("dev")
    owners = lax.dynamic_slice_in_dim(panel_owner, group, 1, 0)[0]
    sources = block_sources(dev)

    border_blocks = gather_blocks(border.T)

    stored = panels[0]
    chunks = jnp.where(
        owners[1] == dev,
        jnp.pad(stored[512:].reshape(16, 64, 512), ((0, 0), (0, 32), (0, 0))),
        jnp.where(
            owners[2] == dev,
            jnp.pad(stored[1024:].reshape(16, 32, 512), ((0, 0), (0, 64), (0, 0))),
            stored.reshape(16, 96, 512),
        ),
    )
    received = lax.all_to_all(chunks, "dev", 0, 0, tiled=True)
    piece = jnp.concatenate(
        [
            lax.dynamic_slice(received, (owners[step], 0, 0), (1, 96 - 32 * step, 512))[0]
            for step in range(3)
        ],
        axis=0,
    )
    panel_blocks = gather_blocks(piece)
    answer = solve(panel_blocks, sources, interface_cols)
    tile = make_tile(border_blocks, sources, answer)

    y, z_hi, core = group // 4, (group // 2) % 2, group % 2
    pair = lax.dynamic_slice_in_dim(block_rows, (group // 2) * 2, 2, 0)
    mine_first = jnp.where(core == 0, pair, pair[::-1]).reshape(16)
    owner = mine_first // 2
    slot = ((owner // 4 - y) % 4) * 4 + ((owner // 2) % 2 ^ z_hi) * 2 + mine_first % 2
    slots = jnp.where(owner % 2 == core, slot, -1).astype(jnp.int32)
    stay, up1, up2, up3 = place(slots, tile, swap_grp(tile, 1))
    summed = (
        stay.astype(F32)
        + hop_y(up1, 1).astype(F32)
        + hop_y(up2, 2).astype(F32)
        + hop_y(up3, 3).astype(F32)
    )
    own_rows = summed[:2] + swap_grp(summed[2:].astype(BF16), 2).astype(F32)
    masked = own_rows.reshape(2, 128, 2, 128) * pattern.astype(F32)[:, None, :, None]
    schur = masked.reshape(256, 256).astype(BF16)

    x = dev % 4
    partial = jnp.dot(schur, block_x, preferred_element_type=F32).astype(BF16).reshape(4, 64, 256)

    def quarter(dx):
        return lax.dynamic_slice_in_dim(partial, (x + dx) % 4, 1, 0)[0]

    row_sum = quarter(0).astype(F32)
    for dx in (1, 2, 3):
        row_sum += hop_x(quarter(dx), dx).astype(F32)
    row_sum = row_sum.astype(BF16)
    full = row_sum.astype(F32)
    for bits in (1, 2, 3):
        full += hop_z(row_sum, bits).astype(F32)
    full = full.astype(BF16)
    parts = jnp.stack([full] + [hop_x(full, -dx) for dx in (1, 2, 3)])
    twice = jnp.concatenate([parts, parts], axis=0)
    product = lax.dynamic_slice_in_dim(twice, (4 - x) % 4, 4, 0).reshape(256, 256).astype(F32)
    return (schur, product)


def solution(mesh):
    return jax.shard_map(
        local,
        mesh=mesh,
        in_specs=(
            P(("grp", "dev"), None, None),
            P(),
            P(None, ("grp", "dev")),
            P("grp", "dev"),
            P(),
            P("grp", "dev"),
            P("dev", None),
        ),
        out_specs=(P("grp", "dev"), P("grp", None)),
        check_vma=False,
    )
```

```python
import functools

import jax
import jax.numpy as jnp
from jax import lax
from jax.experimental import pallas as pl
from jax.experimental.pallas import tpu as pltpu
from jax.sharding import PartitionSpec as P

F32 = jnp.float32
BF16 = jnp.bfloat16
ANY = pl.BlockSpec(memory_space=pl.ANY)
VMEM = pl.BlockSpec(memory_space=pltpu.VMEM)
SMEM = pl.BlockSpec(memory_space=pltpu.SMEM)


def hop_x(value, dx):
    perm = [(z * 4 + x, z * 4 + (x + dx) % 4) for z in range(4) for x in range(4)]
    return lax.ppermute(value, "dev", perm)


def hop_z(value, bits):
    perm = [(z * 4 + x, (z ^ bits) * 4 + x) for z in range(4) for x in range(4)]
    return lax.ppermute(value, "dev", perm)


def hop_y(value, dy):
    perm = [(y * 4 + r, ((y + dy) % 4) * 4 + r) for y in range(4) for r in range(4)]
    return lax.ppermute(value, "grp", perm)


def swap_grp(value, bits):
    return lax.ppermute(value, "grp", [(g, g ^ bits) for g in range(16)])


def gather_blocks(block):
    low = jnp.stack([block, hop_z(block, 1)])
    high = jnp.stack([hop_z(block, 2), hop_z(block, 3)])
    low_left = hop_x(low, 1)
    high_right = hop_x(high, -1)
    high_left = hop_x(high, 1)
    low_right = hop_x(low, -1)
    low_far = hop_x(low_left, 1)
    high_far = hop_x(high_right, -1)
    return [low, high, low_left, high_left, low_right, high_right, low_far, high_far]


def block_sources(dev):
    z, x = dev // 4, dev % 4
    order = []
    for dx in (0, 3, 1, 2):
        for bits in range(4):
            order.append((z ^ bits) * 4 + (x + dx) % 4)
    return jnp.stack(order).astype(jnp.int32)


HEIGHTS = (80, 48, 16)
OFFSETS = (0, 80, 128)
PIECE = 144


def pack_kernel(info, slot, *refs):
    outs, (held, load_sem, sem) = refs[:4], refs[4:]
    x, z = info[1], info[2]
    row = lax.broadcasted_iota(jnp.int32, (256, 256), 0)
    col = lax.broadcasted_iota(jnp.int32, (256, 256), 1)
    for step in range(3):

        @pl.when(info[0] == step)
        def _():
            top = 512 * step
            load = pltpu.make_async_copy(slot.at[0, pl.ds(top, 1536 - top)], held.at[pl.ds(top, 1536 - top)], load_sem)
            load.start()
            load.wait()
            first = held[top : top + 256, :256].astype(F32)
            second = held[top + 256 : top + 512, 256:].astype(F32).T
            held[top + 256 : top + 512, 256:] = jnp.where(row > col, first, second).astype(BF16)
            height = HEIGHTS[step]
            copies = []
            for dx in range(4):
                for bits in range(4):
                    chunk = (z ^ bits) * 4 + (x + dx) % 4
                    start = pl.multiple_of(top + 256 + chunk * height, 16)
                    copies.append(
                        pltpu.make_async_copy(
                            held.at[pl.ds(start, height)],
                            outs[dx].at[bits, pl.ds(0, height)],
                            sem.at[dx * 4 + bits],
                        )
                    )
            for copy in copies:
                copy.start()
            for copy in copies:
                copy.wait()


def pack(info, panels):
    return pl.pallas_call(
        pack_kernel,
        out_shape=[jax.ShapeDtypeStruct((4, HEIGHTS[0], 512), BF16)] * 4,
        in_specs=[SMEM, ANY],
        out_specs=[ANY] * 4,
        scratch_shapes=[
            pltpu.VMEM((1536, 512), BF16),
            pltpu.SemaphoreType.DMA,
            pltpu.SemaphoreType.DMA((16,)),
        ],
        cost_estimate=pl.CostEstimate(flops=1_000_000, bytes_accessed=2_800_000, transcendentals=0),
        compiler_params=pltpu.CompilerParams(vmem_limit_bytes=16 << 20),
        name="pack",
    )(info, panels)


def pick_kernel(picks, *refs):
    chunks, outs, sem = refs[:4], refs[4:8], refs[8]

    def each(act):
        for step in range(3):
            for dx in range(4):

                @pl.when(picks[step] == dx)
                def _():
                    for bits in range(4):
                        act(
                            pltpu.make_async_copy(
                                chunks[dx].at[bits, pl.ds(0, HEIGHTS[step])],
                                outs[bits].at[pl.ds(OFFSETS[step], HEIGHTS[step])],
                                sem.at[step * 4 + bits],
                            )
                        )

    each(lambda copy: copy.start())
    each(lambda copy: copy.wait())


def pick(picks, chunks):
    return pl.pallas_call(
        pick_kernel,
        out_shape=[jax.ShapeDtypeStruct((PIECE, 512), BF16)] * 4,
        in_specs=[SMEM] + [ANY] * 4,
        out_specs=[VMEM] * 4,
        scratch_shapes=[pltpu.SemaphoreType.DMA((12,))],
        cost_estimate=pl.CostEstimate(flops=1_000_000, bytes_accessed=1_200_000, transcendentals=0),
        compiler_params=pltpu.CompilerParams(vmem_limit_bytes=8 << 20),
        name="pick",
    )(picks, *chunks)


def solve_kernel(sources, *refs):
    blocks, (cols, out, pan0, pan1, pan2, sem) = refs[:8], refs[8:]
    half = 256
    copies = []
    for part in range(16):
        block = blocks[part // 2].at[part % 2]
        source = sources[part]
        for step, pan in enumerate((pan0, pan1, pan2)):
            rows = HEIGHTS[step]
            start = pl.multiple_of(source * rows, 16)
            copies.append(
                pltpu.make_async_copy(
                    block.at[pl.ds(OFFSETS[step], rows)], pan.at[pl.ds(start, rows)], sem.at[part * 3 + step]
                )
            )
    for copy in copies:
        copy.start()
    for copy in copies:
        copy.wait()
    row = lax.broadcasted_iota(jnp.int32, (half, half), 0)
    col = lax.broadcasted_iota(jnp.int32, (half, half), 1)

    def dot(a, b):
        return jnp.dot(a, b, preferred_element_type=F32)

    def unit(below):
        return jnp.where(row > col, below, jnp.where(row == col, 1.0, 0.0)).astype(BF16)

    def inverse_times(pan, current):
        shared = pan[:half, half:].astype(F32)
        high, low = current[:half], current[half:]
        upper = dot(unit(shared), high)
        lower = dot(pan[:half, :half], high) + dot(unit(shared.T), low)
        return jnp.concatenate([upper, lower], axis=0).astype(BF16)

    first = inverse_times(pan0, cols[:512])
    out[:512] = first
    rest = cols[512:].astype(F32) - dot(pan0[half:], first)
    second = inverse_times(pan1, rest[:512].astype(BF16))
    out[512:1024] = second
    rest = rest[512:] - dot(pan1[half:], second)
    out[1024:] = inverse_times(pan2, rest.astype(BF16))


def solve(blocks, sources, cols):
    return pl.pallas_call(
        solve_kernel,
        out_shape=jax.ShapeDtypeStruct((1536, 256), BF16),
        in_specs=[SMEM] + [ANY] * 8 + [VMEM],
        out_specs=VMEM,
        scratch_shapes=[
            pltpu.VMEM((1280, 512), BF16),
            pltpu.VMEM((768, 512), BF16),
            pltpu.VMEM((256, 512), BF16),
            pltpu.SemaphoreType.DMA((48,)),
        ],
        cost_estimate=pl.CostEstimate(flops=800_000_000, bytes_accessed=5_000_000, transcendentals=0),
        compiler_params=pltpu.CompilerParams(vmem_limit_bytes=32 << 20),
        name="solve",
    )(sources, *blocks, cols)


def tile_kernel(sources, *refs):
    blocks, (answer, out, border, sem) = refs[:8], refs[8:]
    copies = []
    for part in range(16):
        start = pl.multiple_of(sources[part] * 96, 96)
        copies.append(
            pltpu.make_async_copy(
                blocks[part // 2].at[part % 2], border.at[pl.ds(start, 96)], sem.at[part]
            )
        )
    for copy in copies:
        copy.start()
    for copy in copies:
        copy.wait()
    for block in range(4):
        part = border[:, block * 256 : (block + 1) * 256]
        tile = lax.dot_general(part, answer[...], (((0,), (0,)), ((), ())), preferred_element_type=F32)
        out[2 * block : 2 * block + 2] = tile.reshape(2, 128, 256).astype(BF16)


def make_tile(blocks, sources, answer):
    return pl.pallas_call(
        tile_kernel,
        out_shape=jax.ShapeDtypeStruct((8, 128, 256), BF16),
        in_specs=[SMEM] + [ANY] * 8 + [VMEM],
        out_specs=VMEM,
        scratch_shapes=[pltpu.VMEM((1536, 1024), BF16), pltpu.SemaphoreType.DMA((16,))],
        cost_estimate=pl.CostEstimate(flops=800_000_000, bytes_accessed=5_000_000, transcendentals=0),
        compiler_params=pltpu.CompilerParams(vmem_limit_bytes=32 << 20),
        name="tile",
    )(sources, *blocks, answer)


def place_kernel(slots, own, other, stay, up1, up2, up3, total):
    total[...] = jnp.zeros_like(total)
    for part in range(16):
        source = own if part < 8 else other
        slot = slots[part]

        @pl.when(slot >= 0)
        def _():
            total[slot] += source[part % 8].astype(F32)

    for index, out in enumerate((stay, up1, up2, up3)):
        out[...] = total[index * 4 : index * 4 + 4].astype(BF16)


def place(slots, own, other):
    return pl.pallas_call(
        place_kernel,
        out_shape=[jax.ShapeDtypeStruct((4, 128, 256), BF16)] * 4,
        in_specs=[SMEM, VMEM, VMEM],
        out_specs=[VMEM] * 4,
        scratch_shapes=[pltpu.VMEM((16, 128, 256), F32)],
        cost_estimate=pl.CostEstimate(flops=1_000_000, bytes_accessed=2_000_000, transcendentals=0),
        compiler_params=pltpu.CompilerParams(vmem_limit_bytes=32 << 20),
        name="place",
    )(slots, own, other)


def local(panels, panel_owner, interface_cols, border, block_rows, pattern, block_x):
    group = lax.axis_index("grp")
    dev = lax.axis_index("dev")
    owners = lax.dynamic_slice_in_dim(panel_owner, group, 1, 0)[0]
    sources = block_sources(dev)

    border_blocks = gather_blocks(border.T)

    z, x = dev // 4, dev % 4
    held = jnp.where(owners[0] == dev, 0, jnp.where(owners[1] == dev, 1, jnp.where(owners[2] == dev, 2, 3)))
    chunks = pack(jnp.stack([held, x, z]).astype(jnp.int32), panels)
    chunks = [chunks[0]] + [hop_x(chunks[dx], dx) for dx in (1, 2, 3)]
    picks = jnp.where(owners // 4 == z, (x - owners) % 4, 4).astype(jnp.int32)
    pieces = pick(picks, chunks)
    pieces = [pieces[0]] + [hop_z(pieces[bits], bits) for bits in (1, 2, 3)]
    from_z = jnp.repeat(owners // 4 ^ z, jnp.array(HEIGHTS), total_repeat_length=PIECE)[:, None]
    piece = pieces[3]
    for bits in (0, 1, 2):
        piece = jnp.where(from_z == bits, pieces[bits], piece)
    panel_blocks = gather_blocks(piece)
    answer = solve(panel_blocks, sources, interface_cols)
    tile = make_tile(border_blocks, sources, answer)

    y, z_hi, core = group // 4, (group // 2) % 2, group % 2
    pair = lax.dynamic_slice_in_dim(block_rows, (group // 2) * 2, 2, 0)
    mine_first = jnp.where(core == 0, pair, pair[::-1]).reshape(16)
    owner = mine_first // 2
    slot = ((owner // 4 - y) % 4) * 4 + ((owner // 2) % 2 ^ z_hi) * 2 + mine_first % 2
    slots = jnp.where(owner % 2 == core, slot, -1).astype(jnp.int32)
    stay, up1, up2, up3 = place(slots, tile, swap_grp(tile, 1))
    summed = (
        stay.astype(F32)
        + hop_y(up1, 1).astype(F32)
        + hop_y(up2, 2).astype(F32)
        + hop_y(up3, 3).astype(F32)
    )
    own_rows = summed[:2] + swap_grp(summed[2:].astype(BF16), 2).astype(F32)
    masked = own_rows.reshape(2, 128, 2, 128) * pattern.astype(F32)[:, None, :, None]
    schur = masked.reshape(256, 256).astype(BF16)

    partial = jnp.dot(schur, block_x, preferred_element_type=F32).astype(BF16).reshape(4, 64, 256)

    def quarter(dx):
        return lax.dynamic_slice_in_dim(partial, (x + dx) % 4, 1, 0)[0]

    row_sum = quarter(0).astype(F32)
    for dx in (1, 2, 3):
        row_sum += hop_x(quarter(dx), dx).astype(F32)
    row_sum = row_sum.astype(BF16)
    full = row_sum.astype(F32)
    for bits in (1, 2, 3):
        full += hop_z(row_sum, bits).astype(F32)
    full = full.astype(BF16)
    parts = jnp.stack([full] + [hop_x(full, -dx) for dx in (1, 2, 3)])
    twice = jnp.concatenate([parts, parts], axis=0)
    product = lax.dynamic_slice_in_dim(twice, (4 - x) % 4, 4, 0).reshape(256, 256).astype(F32)
    return (schur, product)


def solution(mesh):
    return jax.shard_map(
        local,
        mesh=mesh,
        in_specs=(
            P(("grp", "dev"), None, None),
            P(),
            P(None, ("grp", "dev")),
            P("grp", "dev"),
            P(),
            P("grp", "dev"),
            P("dev", None),
        ),
        out_specs=(P("grp", "dev"), P("grp", None)),
        check_vma=False,
    )
```

```python
import jax
import jax.numpy as jnp
from jax import lax
from jax.experimental import pallas as pl
from jax.experimental.pallas import tpu as pltpu
from jax.sharding import PartitionSpec as P


F32 = jnp.float32
BF16 = jnp.bfloat16
ANY = pl.BlockSpec(memory_space=pl.ANY)
VMEM = pl.BlockSpec(memory_space=pltpu.VMEM)
SMEM = pl.BlockSpec(memory_space=pltpu.SMEM)


def hop_x(value, dx):
    perm = [(z * 4 + x, z * 4 + (x + dx) % 4) for z in range(4) for x in range(4)]
    return lax.ppermute(value, "dev", perm)


def hop_z(value, bits):
    perm = [(z * 4 + x, (z ^ bits) * 4 + x) for z in range(4) for x in range(4)]
    return lax.ppermute(value, "dev", perm)


def hop_y(value, dy):
    perm = [(y * 4 + r, ((y + dy) % 4) * 4 + r) for y in range(4) for r in range(4)]
    return lax.ppermute(value, "grp", perm)


def swap_grp(value, bits):
    return lax.ppermute(value, "grp", [(g, g ^ bits) for g in range(16)])


def gather_blocks(block):
    near = [hop_z(block, bits) for bits in (1, 2, 3)]
    low = jnp.stack([block, near[0]])
    high = jnp.stack([near[1], near[2]])
    low_left = hop_x(low, 1)
    high_right = hop_x(high, -1)
    high_left = hop_x(high, 1)
    low_right = hop_x(low, -1)
    low_far = hop_x(low_left, 1)
    high_far = hop_x(high_right, -1)
    return [low, high, low_left, high_left, low_right, high_right, low_far, high_far]


def block_source(part):
    dev = lax.axis_index("dev")
    return ((dev >> 2) ^ (part % 4)) * 4 + ((dev + (0, 3, 1, 2)[part // 4]) & 3)


HEIGHTS = (80, 48, 16)
OFFSETS = (0, 80, 128)
PIECE = 144


def pack_kernel(owners, slot, *refs):
    outs, (held, load_sem, sem) = refs[:4], refs[4:]
    group, dev = lax.axis_index("grp"), lax.axis_index("dev")
    x, z = dev & 3, dev >> 2
    row = lax.broadcasted_iota(jnp.int32, (256, 256), 0)
    col = lax.broadcasted_iota(jnp.int32, (256, 256), 1)
    for step in range(3):

        @pl.when(owners[group, step] == dev)
        def _():
            top = 512 * step
            load = pltpu.make_async_copy(slot.at[0, pl.ds(top, 1536 - top)], held.at[pl.ds(top, 1536 - top)], load_sem)
            load.start()
            load.wait()
            first = held[top : top + 256, :256].astype(F32)
            second = held[top + 256 : top + 512, 256:].astype(F32).T
            held[top + 256 : top + 512, 256:] = jnp.where(row > col, first, second).astype(BF16)
            height = HEIGHTS[step]
            copies = []
            for dx in range(4):
                for bits in range(4):
                    chunk = (z ^ bits) * 4 + ((x + dx) & 3)
                    start = pl.multiple_of(top + 256 + chunk * height, 16)
                    copies.append(
                        pltpu.make_async_copy(
                            held.at[pl.ds(start, height)],
                            outs[dx].at[bits, pl.ds(0, height)],
                            sem.at[dx * 4 + bits],
                        )
                    )
            for copy in copies:
                copy.start()
            for copy in copies:
                copy.wait()


def pack(owners, panels):
    return pl.pallas_call(
        pack_kernel,
        out_shape=[jax.ShapeDtypeStruct((4, HEIGHTS[0], 512), BF16)] * 4,
        in_specs=[SMEM, ANY],
        out_specs=[ANY] * 4,
        scratch_shapes=[
            pltpu.VMEM((1536, 512), BF16),
            pltpu.SemaphoreType.DMA,
            pltpu.SemaphoreType.DMA((16,)),
        ],
        cost_estimate=pl.CostEstimate(flops=1_000_000, bytes_accessed=2_800_000, transcendentals=0),
        compiler_params=pltpu.CompilerParams(vmem_limit_bytes=16 << 20),
        name="pack",
    )(owners, panels)


def pick_kernel(owners, *refs):
    chunks, outs, sem = refs[:4], refs[4:8], refs[8]
    group, dev = lax.axis_index("grp"), lax.axis_index("dev")

    def each(act):
        for step in range(3):
            owner = owners[group, step]
            for dx in range(4):

                @pl.when(owner == (dev >> 2) * 4 + ((dev - dx) & 3))
                def _():
                    for bits in range(4):
                        act(
                            pltpu.make_async_copy(
                                chunks[dx].at[bits, pl.ds(0, HEIGHTS[step])],
                                outs[bits].at[pl.ds(OFFSETS[step], HEIGHTS[step])],
                                sem.at[step * 4 + bits],
                            )
                        )

    each(lambda copy: copy.start())
    each(lambda copy: copy.wait())


def pick(owners, chunks):
    return pl.pallas_call(
        pick_kernel,
        out_shape=[jax.ShapeDtypeStruct((PIECE, 512), BF16)] * 4,
        in_specs=[SMEM] + [ANY] * 4,
        out_specs=[VMEM] * 4,
        scratch_shapes=[pltpu.SemaphoreType.DMA((12,))],
        cost_estimate=pl.CostEstimate(flops=1_000_000, bytes_accessed=1_200_000, transcendentals=0),
        compiler_params=pltpu.CompilerParams(vmem_limit_bytes=8 << 20),
        name="pick",
    )(owners, *chunks)


def tile_kernel(*refs):
    panels, strips, (cols, out, pan0, pan1, pan2, border, answer, sem) = refs[:8], refs[8:16], refs[16:]
    half = 256
    pans = (pan0, pan1, pan2)
    copies = [[], [], [], []]
    for part in range(16):
        source = block_source(part)
        for step in range(3):
            rows = HEIGHTS[step]
            start = pl.multiple_of(source * rows, 16)
            copies[step].append(
                pltpu.make_async_copy(
                    panels[part // 2].at[part % 2, pl.ds(OFFSETS[step], rows)],
                    pans[step].at[pl.ds(start, rows)],
                    sem.at[part * 4 + step],
                )
            )
        start = pl.multiple_of(source * 96, 32)
        copies[3].append(
            pltpu.make_async_copy(
                strips[part // 2].at[part % 2], border.at[pl.ds(start, 96)], sem.at[part * 4 + 3]
            )
        )
    for group in copies:
        for copy in group:
            copy.start()
    row = lax.broadcasted_iota(jnp.int32, (half, half), 0)
    col = lax.broadcasted_iota(jnp.int32, (half, half), 1)

    def dot(a, b):
        return jnp.dot(a, b, preferred_element_type=F32)

    def unit(below):
        return jnp.where(row > col, below, jnp.where(row == col, 1.0, 0.0)).astype(BF16)

    def inverse_times(step, current):
        pan = pans[step]
        for copy in copies[step]:
            copy.wait()
        shared = pan[:half, half:].astype(F32)
        high, low = current[:half], current[half:]
        upper = dot(unit(shared), high)
        lower = dot(pan[:half, :half], high) + dot(unit(shared.T), low)
        result = jnp.concatenate([upper, lower], axis=0).astype(BF16)
        answer[step * 512 : step * 512 + 512] = result
        return result

    first = inverse_times(0, cols[:512])
    rest = cols[512:].astype(F32) - dot(pan0[half:], first)
    second = inverse_times(1, rest[:512].astype(BF16))
    rest = rest[512:] - dot(pan1[half:], second)
    inverse_times(2, rest.astype(BF16))
    for copy in copies[3]:
        copy.wait()
    tile = lax.dot_general(answer[...], border[...], (((0,), (0,)), ((), ())), preferred_element_type=F32)
    for block in range(8):
        out[block] = tile[:, block * 128 : block * 128 + 128].astype(BF16)


def make_tile(panels, strips, cols):
    return pl.pallas_call(
        tile_kernel,
        out_shape=jax.ShapeDtypeStruct((8, 256, 128), BF16),
        in_specs=[ANY] * 16 + [VMEM],
        out_specs=VMEM,
        scratch_shapes=[
            pltpu.VMEM((1280, 512), BF16),
            pltpu.VMEM((768, 512), BF16),
            pltpu.VMEM((256, 512), BF16),
            pltpu.VMEM((1536, 1024), BF16),
            pltpu.VMEM((1536, 256), BF16),
            pltpu.SemaphoreType.DMA((64,)),
        ],
        cost_estimate=pl.CostEstimate(flops=1_500_000_000, bytes_accessed=8_000_000, transcendentals=0),
        compiler_params=pltpu.CompilerParams(vmem_limit_bytes=32 << 20),
        name="tile",
    )(*panels, *strips, cols)


def place_kernel(block_rows, own, other, *refs):
    outs, total = refs[:8], refs[8]
    group = lax.axis_index("grp")
    core = group & 1
    total[...] = jnp.zeros_like(total)
    for part in range(16):
        source, giver = (own, group) if part < 8 else (other, group ^ 1)
        target = block_rows[giver, part % 8]
        owner = target >> 1
        slot = (((owner >> 2) - (group >> 2)) & 3) * 4 + (((owner ^ group) >> 1) & 1) * 2 + (target & 1)

        @pl.when((owner & 1) == core)
        def _():
            total[slot] += source[part % 8].astype(F32)

    for dy in range(4):
        for half in range(2):
            outs[half * 4 + dy][...] = total[dy * 4 + half * 2 : dy * 4 + half * 2 + 2].astype(BF16)


def place(block_rows, own, other):
    return pl.pallas_call(
        place_kernel,
        out_shape=[jax.ShapeDtypeStruct((2, 256, 128), BF16)] * 8,
        in_specs=[SMEM, VMEM, VMEM],
        out_specs=[VMEM] * 8,
        scratch_shapes=[pltpu.VMEM((16, 256, 128), F32)],
        cost_estimate=pl.CostEstimate(flops=1_000_000, bytes_accessed=2_000_000, transcendentals=0),
        compiler_params=pltpu.CompilerParams(vmem_limit_bytes=32 << 20),
        name="place",
    )(block_rows, own, other)


def add_y(parts):
    moved = [part.astype(F32) for part in [parts[0]] + [hop_y(parts[dy], dy) for dy in (1, 2, 3)]]
    return (moved[0] + moved[2]) + (moved[1] + moved[3])


def step(panels, panel_owner, interface_cols, border, block_rows, pattern, block_x):
    group = lax.axis_index("grp")
    dev = lax.axis_index("dev")

    strips = gather_blocks(border.T)

    chunks = pack(panel_owner, panels)
    chunks = [chunks[0]] + [hop_x(chunks[dx], dx) for dx in (1, 2, 3)]
    pieces = pick(panel_owner, chunks)
    pieces = [pieces[0]] + [hop_z(pieces[bits], bits) for bits in (1, 2, 3)]
    owners = lax.dynamic_slice_in_dim(panel_owner, group, 1, 0)[0]
    near = owners // 4 ^ dev // 4
    row = lax.broadcasted_iota(jnp.int32, (PIECE, 1), 0)
    from_z = jnp.where(row < OFFSETS[1], near[0], jnp.where(row < OFFSETS[2], near[1], near[2]))
    piece = pieces[3]
    for bits in (0, 1, 2):
        piece = jnp.where(from_z == bits, pieces[bits], piece)
    tile = make_tile(gather_blocks(piece), strips, interface_cols)

    placed = place(block_rows, tile, swap_grp(tile, 1))
    other = add_y(placed[4:])
    mine = add_y(placed[:4])
    other = swap_grp(other.astype(BF16), 2)
    own_rows = (mine + other.astype(F32)).transpose(0, 2, 1)
    masked = own_rows.reshape(2, 128, 2, 128) * pattern.astype(F32)[:, None, :, None]
    schur = masked.reshape(256, 256).astype(BF16)

    partial = jnp.dot(schur, block_x, preferred_element_type=F32).astype(BF16)
    moved = [part.astype(F32) for part in [partial] + [hop_x(partial, dx) for dx in (1, 2, 3)]]
    row_sum = ((moved[0] + moved[2]) + (moved[1] + moved[3])).astype(BF16)
    moved = [part.astype(F32) for part in [row_sum] + [hop_z(row_sum, bits) for bits in (1, 2, 3)]]
    product = (moved[0] + moved[1]) + (moved[2] + moved[3])
    return (schur, product)


def solution(mesh):
    return jax.shard_map(
        step,
        mesh=mesh,
        in_specs=(
            P(("grp", "dev"), None, None),
            P(),
            P(None, ("grp", "dev")),
            P("grp", "dev"),
            P(),
            P("grp", "dev"),
            P("dev", None),
        ),
        out_specs=(P("grp", "dev"), P("grp", None)),
        check_vma=False,
    )
```

```python
import jax
import jax.numpy as jnp
from jax import lax
from jax.experimental import pallas as pl
from jax.experimental.pallas import tpu as pltpu
from jax.sharding import PartitionSpec as P


F32 = jnp.float32
BF16 = jnp.bfloat16
VMEM = pl.BlockSpec(memory_space=pltpu.VMEM)
SMEM = pl.BlockSpec(memory_space=pltpu.SMEM)


def hop_x(value, dx):
    perm = [(z * 4 + x, z * 4 + (x + dx) % 4) for z in range(4) for x in range(4)]
    return lax.ppermute(value, "dev", perm)


def hop_z(value, bits):
    perm = [(z * 4 + x, (z ^ bits) * 4 + x) for z in range(4) for x in range(4)]
    return lax.ppermute(value, "dev", perm)


def hop_y(value, dy):
    perm = [(y * 4 + r, ((y + dy) % 4) * 4 + r) for y in range(4) for r in range(4)]
    return lax.ppermute(value, "grp", perm)


def swap_grp(value, bits):
    return lax.ppermute(value, "grp", [(g, g ^ bits) for g in range(16)])


def gather_blocks(block):
    near = [hop_z(block, bits) for bits in (1, 2, 3)]
    low = jnp.stack([block, near[0]])
    high = jnp.stack([near[1], near[2]])
    low_left = hop_x(low, 1)
    high_right = hop_x(high, -1)
    high_left = hop_x(high, 1)
    low_right = hop_x(low, -1)
    low_far = hop_x(low_left, 1)
    high_far = hop_x(high_right, -1)
    return [low, high, low_left, high_left, low_right, high_right, low_far, high_far]


def block_source(part):
    dev = lax.axis_index("dev")
    return ((dev >> 2) ^ (part % 4)) * 4 + ((dev + (0, 3, 1, 2)[part // 4]) & 3)


HEIGHTS = (80, 48, 16)
OFFSETS = (0, 80, 128)
PIECE = 144


def pack_kernel(owners, slot, *refs):
    outs, (held, sem) = refs[:4], refs[4:]
    group, dev = lax.axis_index("grp"), lax.axis_index("dev")
    row = lax.broadcasted_iota(jnp.int32, (256, 256), 0)
    col = lax.broadcasted_iota(jnp.int32, (256, 256), 1)
    for step in range(3):

        @pl.when(owners[step, group] == dev)
        def _():
            top = 512 * step
            load = pltpu.make_async_copy(
                slot.at[0, pl.ds(top, 1536 - top)], held.at[pl.ds(top, 1536 - top)], sem
            )
            load.start()
            load.wait()
            first = held[top : top + 256, :256].astype(F32)
            second = held[top + 256 : top + 512, 256:].astype(F32).T
            held[top + 256 : top + 512, 256:] = jnp.where(row > col, first, second).astype(BF16)
            height = HEIGHTS[step]
            for dx in range(4):
                for bits in range(4):
                    chunk = ((dev >> 2) ^ bits) * 4 + ((dev + dx) & 3)
                    start = pl.multiple_of(top + 256 + chunk * height, 16)
                    outs[dx][bits, :height] = held[pl.ds(start, height)]


def pack(owners, panels):
    return pl.pallas_call(
        pack_kernel,
        out_shape=[jax.ShapeDtypeStruct((4, HEIGHTS[0], 512), BF16)] * 4,
        in_specs=[SMEM, pl.BlockSpec(memory_space=pltpu.HBM)],
        out_specs=[VMEM] * 4,
        scratch_shapes=[pltpu.VMEM((1536, 512), BF16), pltpu.SemaphoreType.DMA],
        cost_estimate=pl.CostEstimate(flops=1_000_000, bytes_accessed=2_800_000, transcendentals=0),
        compiler_params=pltpu.CompilerParams(vmem_limit_bytes=16 << 20),
        name="pack",
    )(owners, panels)


def pick_kernel(owners, *refs):
    chunks, outs = refs[:4], refs[4:]
    group, dev = lax.axis_index("grp"), lax.axis_index("dev")
    for step in range(3):
        first, rows = OFFSETS[step], HEIGHTS[step]
        owner = owners[step, group]
        for dx in range(4):

            @pl.when(owner == (dev >> 2) * 4 + ((dev - dx) & 3))
            def _():
                for bits in range(4):
                    outs[bits][first : first + rows] = chunks[dx][bits, :rows]


def pick(owners, chunks):
    return pl.pallas_call(
        pick_kernel,
        out_shape=[jax.ShapeDtypeStruct((PIECE, 512), BF16)] * 4,
        in_specs=[SMEM] + [VMEM] * 4,
        out_specs=[VMEM] * 4,
        cost_estimate=pl.CostEstimate(flops=1_000_000, bytes_accessed=1_200_000, transcendentals=0),
        compiler_params=pltpu.CompilerParams(vmem_limit_bytes=8 << 20),
        name="pick",
    )(owners, *chunks)


def tile_kernel(*refs):
    panels, strips, (cols, out, pan0, pan1, pan2, border, answer) = refs[:8], refs[8:16], refs[16:]
    half = 256
    pans = (pan0, pan1, pan2)
    sources = [block_source(part) for part in range(16)]
    row = lax.broadcasted_iota(jnp.int32, (half, half), 0)
    col = lax.broadcasted_iota(jnp.int32, (half, half), 1)

    def dot(a, b):
        return jnp.dot(a, b, preferred_element_type=F32)

    def unit(below):
        return jnp.where(row > col, below, jnp.where(row == col, 1.0, 0.0)).astype(BF16)

    def inverse_times(step, current):
        pan, first, rows = pans[step], OFFSETS[step], HEIGHTS[step]
        for part, source in enumerate(sources):
            pan[pl.ds(pl.multiple_of(source * rows, 16), rows)] = panels[part // 2][part % 2, first : first + rows]
        shared = pan[:half, half:].astype(F32)
        high, low = current[:half], current[half:]
        upper = dot(unit(shared), high)
        lower = dot(pan[:half, :half], high) + dot(unit(shared.T), low)
        result = jnp.concatenate([upper, lower], axis=0).astype(BF16)
        answer[step * 512 : step * 512 + 512] = result
        return result

    first = inverse_times(0, cols[:512])
    rest = cols[512:].astype(F32) - dot(pan0[half:], first)
    second = inverse_times(1, rest[:512].astype(BF16))
    rest = rest[512:] - dot(pan1[half:], second)
    inverse_times(2, rest.astype(BF16))
    for part, source in enumerate(sources):
        border[pl.ds(pl.multiple_of(source * 96, 32), 96)] = strips[part // 2][part % 2]
    tile = lax.dot_general(answer[...], border[...], (((0,), (0,)), ((), ())), preferred_element_type=F32)
    for block in range(8):
        out[block] = tile[:, block * 128 : block * 128 + 128].astype(BF16)


def make_tile(panels, strips, cols):
    return pl.pallas_call(
        tile_kernel,
        out_shape=jax.ShapeDtypeStruct((8, 256, 128), BF16),
        in_specs=[VMEM] * 17,
        out_specs=VMEM,
        scratch_shapes=[
            pltpu.VMEM((1280, 512), BF16),
            pltpu.VMEM((768, 512), BF16),
            pltpu.VMEM((256, 512), BF16),
            pltpu.VMEM((1536, 1024), BF16),
            pltpu.VMEM((1536, 256), BF16),
        ],
        cost_estimate=pl.CostEstimate(flops=1_500_000_000, bytes_accessed=8_000_000, transcendentals=0),
        compiler_params=pltpu.CompilerParams(vmem_limit_bytes=32 << 20),
        name="tile",
    )(*panels, *strips, cols)


def place_kernel(block_rows, own, other, *refs):
    outs, total = refs[:8], refs[8]
    group = lax.axis_index("grp")
    core = group & 1
    total[...] = jnp.zeros_like(total)
    for part in range(16):
        source, giver = (own, group) if part < 8 else (other, group ^ 1)
        target = block_rows[part % 8, giver]
        owner = target >> 1
        slot = (((owner >> 2) - (group >> 2)) & 3) * 4 + (((owner ^ group) >> 1) & 1) * 2 + (target & 1)

        @pl.when((owner & 1) == core)
        def _():
            total[slot] += source[part % 8].astype(F32)

    for dy in range(4):
        for half in range(2):
            outs[half * 4 + dy][...] = total[dy * 4 + half * 2 : dy * 4 + half * 2 + 2].astype(BF16)


def place(block_rows, own, other):
    return pl.pallas_call(
        place_kernel,
        out_shape=[jax.ShapeDtypeStruct((2, 256, 128), BF16)] * 8,
        in_specs=[SMEM, VMEM, VMEM],
        out_specs=[VMEM] * 8,
        scratch_shapes=[pltpu.VMEM((16, 256, 128), F32)],
        cost_estimate=pl.CostEstimate(flops=1_000_000, bytes_accessed=2_000_000, transcendentals=0),
        compiler_params=pltpu.CompilerParams(vmem_limit_bytes=32 << 20),
        name="place",
    )(block_rows, own, other)


def add_y(parts):
    moved = [part.astype(F32) for part in [parts[0]] + [hop_y(parts[dy], dy) for dy in (1, 2, 3)]]
    return (moved[0] + moved[2]) + (moved[1] + moved[3])


def step(panels, panel_owner, interface_cols, border, block_rows, pattern, block_x):
    group = lax.axis_index("grp")
    dev = lax.axis_index("dev")

    strips = gather_blocks(border.T)

    chunks = pack(panel_owner.T, panels)
    far = hop_x(chunks[2], 2)
    chunks = [chunks[0], hop_x(chunks[1], 1), far, hop_x(chunks[3], 3)]
    pieces = pick(panel_owner.T, chunks)
    pieces = [pieces[0]] + [hop_z(pieces[bits], bits) for bits in (1, 2, 3)]
    owners = lax.dynamic_slice_in_dim(panel_owner, group, 1, 0)[0]
    near = owners // 4 ^ dev // 4
    row = lax.broadcasted_iota(jnp.int32, (PIECE, 1), 0)
    from_z = jnp.where(row < OFFSETS[1], near[0], jnp.where(row < OFFSETS[2], near[1], near[2]))
    piece = pieces[3]
    for bits in (0, 1, 2):
        piece = jnp.where(from_z == bits, pieces[bits], piece)
    tile = make_tile(gather_blocks(piece), strips, interface_cols)

    placed = place(block_rows.T, tile, swap_grp(tile, 1))
    other = add_y(placed[4:])
    mine = add_y(placed[:4])
    other = swap_grp(other.astype(BF16), 2)
    own_rows = (mine + other.astype(F32)).transpose(0, 2, 1)
    masked = own_rows.reshape(2, 128, 2, 128) * pattern.astype(F32)[:, None, :, None]
    schur = masked.reshape(256, 256).astype(BF16)

    partial = jnp.dot(schur, block_x, preferred_element_type=F32).astype(BF16)
    moved = [part.astype(F32) for part in [partial] + [hop_x(partial, dx) for dx in (1, 2, 3)]]
    row_sum = ((moved[0] + moved[2]) + (moved[1] + moved[3])).astype(BF16)
    moved = [part.astype(F32) for part in [row_sum] + [hop_z(row_sum, bits) for bits in (1, 2, 3)]]
    product = (moved[0] + moved[1]) + (moved[2] + moved[3])
    return (schur, product)


def solution(mesh):
    return jax.shard_map(
        step,
        mesh=mesh,
        in_specs=(
            P(("grp", "dev"), None, None),
            P(),
            P(None, ("grp", "dev")),
            P("grp", "dev"),
            P(),
            P("grp", "dev"),
            P("dev", None),
        ),
        out_specs=(P("grp", "dev"), P("grp", None)),
        check_vma=False,
    )
```

```python
import jax
import jax.numpy as jnp
from jax import lax
from jax.experimental import pallas as pl
from jax.experimental.pallas import tpu as pltpu
from jax.sharding import PartitionSpec as P


F32 = jnp.float32
BF16 = jnp.bfloat16
VMEM = pl.BlockSpec(memory_space=pltpu.VMEM)
SMEM = pl.BlockSpec(memory_space=pltpu.SMEM)


def hop_x(value, dx):
    perm = [(z * 4 + x, z * 4 + (x + dx) % 4) for z in range(4) for x in range(4)]
    return lax.ppermute(value, "dev", perm)


def hop_z(value, bits):
    perm = [(z * 4 + x, (z ^ bits) * 4 + x) for z in range(4) for x in range(4)]
    return lax.ppermute(value, "dev", perm)


def hop_y(value, dy):
    perm = [(y * 4 + r, ((y + dy) % 4) * 4 + r) for y in range(4) for r in range(4)]
    return lax.ppermute(value, "grp", perm)


def swap_grp(value, bits):
    return lax.ppermute(value, "grp", [(g, g ^ bits) for g in range(16)])


def pass_kernel(first, second, out_first, out_second):
    out_first[...] = first[...]
    out_second[...] = second[...]


def pass_on(first, second):
    return pl.pallas_call(
        pass_kernel,
        out_shape=[jax.ShapeDtypeStruct(value.shape, value.dtype) for value in (first, second)],
        in_specs=[VMEM] * 2,
        out_specs=[VMEM] * 2,
        cost_estimate=pl.CostEstimate(flops=1_000_000, bytes_accessed=1_600_000, transcendentals=0),
        compiler_params=pltpu.CompilerParams(vmem_limit_bytes=4 << 20),
        name="pass_on",
    )(first, second)


def gather_blocks(block, name):
    near = [hop_z(block, bits) for bits in (1, 2, 3)]
    low = jnp.stack([block, near[0]])
    high = jnp.stack([near[1], near[2]])
    low_left = hop_x(low, 1)
    high_right = hop_x(high, -1)
    high_left = hop_x(high, 1)
    low_right = hop_x(low, -1)
    if name == "border":
        sent_left, sent_right = pass_on(low_left, high_right)
    else:
        sent_left, sent_right = low_left, high_right
    low_far = hop_x(sent_left, 1)
    high_far = hop_x(sent_right, -1)
    return [low, high, low_left, high_left, low_right, high_right, low_far, high_far]


def block_source(part):
    dev = lax.axis_index("dev")
    return ((dev >> 2) ^ (part % 4)) * 4 + ((dev + (0, 3, 1, 2)[part // 4]) & 3)


HEIGHTS = (80, 48, 16)
OFFSETS = (0, 80, 128)
PIECE = 144


def pack_kernel(owners, slot, *refs):
    outs, held = refs[:4], refs[4]
    group, dev = lax.axis_index("grp"), lax.axis_index("dev")
    row = lax.broadcasted_iota(jnp.int32, (256, 256), 0)
    col = lax.broadcasted_iota(jnp.int32, (256, 256), 1)
    for step in range(3):

        @pl.when(owners[step, group] == dev)
        def _():
            top = 512 * step
            held[top + 256 :] = slot[0, top + 256 :]
            first = slot[0, top : top + 256, :256].astype(F32)
            second = slot[0, top + 256 : top + 512, 256:].astype(F32).T
            held[top + 256 : top + 512, 256:] = jnp.where(row > col, first, second).astype(BF16)
            height = HEIGHTS[step]
            for dx in range(4):
                for bits in range(4):
                    chunk = ((dev >> 2) ^ bits) * 4 + ((dev + dx) & 3)
                    start = pl.multiple_of(top + 256 + chunk * height, 16)
                    outs[dx][bits, :height] = held[pl.ds(start, height)]


def pack(owners, panels):
    return pl.pallas_call(
        pack_kernel,
        out_shape=[jax.ShapeDtypeStruct((4, HEIGHTS[0], 512), BF16)] * 4,
        in_specs=[SMEM, VMEM],
        out_specs=[VMEM] * 4,
        scratch_shapes=[pltpu.VMEM((1536, 512), BF16)],
        cost_estimate=pl.CostEstimate(flops=1_000_000, bytes_accessed=2_800_000, transcendentals=0),
        compiler_params=pltpu.CompilerParams(vmem_limit_bytes=16 << 20),
        name="pack",
    )(owners, panels)


def pick_kernel(owners, *refs):
    chunks, outs = refs[:4], refs[4:]
    group, dev = lax.axis_index("grp"), lax.axis_index("dev")
    for step in range(3):
        first, rows = OFFSETS[step], HEIGHTS[step]
        owner = owners[step, group]
        for dx in range(4):

            @pl.when(owner == (dev >> 2) * 4 + ((dev - dx) & 3))
            def _():
                for bits in range(4):
                    outs[bits][first : first + rows] = chunks[dx][bits, :rows]


def pick(owners, chunks):
    return pl.pallas_call(
        pick_kernel,
        out_shape=[jax.ShapeDtypeStruct((PIECE, 512), BF16)] * 4,
        in_specs=[SMEM] + [VMEM] * 4,
        out_specs=[VMEM] * 4,
        cost_estimate=pl.CostEstimate(flops=1_000_000, bytes_accessed=1_200_000, transcendentals=0),
        compiler_params=pltpu.CompilerParams(vmem_limit_bytes=8 << 20),
        name="pick",
    )(owners, *chunks)


def pick_z_kernel(owners, *refs):
    pieces, out = refs[:4], refs[4]
    group, dev = lax.axis_index("grp"), lax.axis_index("dev")
    for step in range(3):
        first, rows = OFFSETS[step], HEIGHTS[step]
        distance = (owners[step, group] ^ dev) >> 2
        for bits in range(4):

            @pl.when(distance == bits)
            def _():
                out[first : first + rows] = pieces[bits][first : first + rows]


def pick_z(owners, pieces):
    return pl.pallas_call(
        pick_z_kernel,
        out_shape=jax.ShapeDtypeStruct((PIECE, 512), BF16),
        in_specs=[SMEM] + [VMEM] * 4,
        out_specs=VMEM,
        cost_estimate=pl.CostEstimate(flops=1_000_000, bytes_accessed=300_000, transcendentals=0),
        compiler_params=pltpu.CompilerParams(vmem_limit_bytes=4 << 20),
        name="pick_z",
    )(owners, *pieces)


def tile_kernel(*refs):
    panels, strips, (cols, out, pan0, pan1, pan2, border, answer) = refs[:8], refs[8:16], refs[16:]
    half = 256
    pans = (pan0, pan1, pan2)
    sources = [block_source(part) for part in range(16)]
    row = lax.broadcasted_iota(jnp.int32, (half, half), 0)
    col = lax.broadcasted_iota(jnp.int32, (half, half), 1)

    def dot(a, b):
        return jnp.dot(a, b, preferred_element_type=F32)

    def unit(below):
        return jnp.where(row > col, below, jnp.where(row == col, 1.0, 0.0)).astype(BF16)

    def inverse_times(step, current):
        pan, first, rows = pans[step], OFFSETS[step], HEIGHTS[step]
        for part, source in enumerate(sources):
            pan[pl.ds(pl.multiple_of(source * rows, 16), rows)] = panels[part // 2][part % 2, first : first + rows]
        shared = pan[:half, half:].astype(F32)
        high, low = current[:half], current[half:]
        upper = dot(unit(shared), high)
        lower = dot(pan[:half, :half], high) + dot(unit(shared.T), low)
        result = jnp.concatenate([upper, lower], axis=0).astype(BF16)
        answer[step * 512 : step * 512 + 512] = result
        return result

    first = inverse_times(0, cols[:512])
    rest = cols[512:].astype(F32) - dot(pan0[half:], first)
    second = inverse_times(1, rest[:512].astype(BF16))
    rest = rest[512:] - dot(pan1[half:], second)
    inverse_times(2, rest.astype(BF16))
    for part, source in enumerate(sources):
        border[pl.ds(pl.multiple_of(source * 96, 32), 96)] = strips[part // 2][part % 2]
    tile = lax.dot_general(answer[...], border[...], (((0,), (0,)), ((), ())), preferred_element_type=F32)
    for block in range(8):
        out[block] = tile[:, block * 128 : block * 128 + 128].astype(BF16)


def make_tile(panels, strips, cols):
    return pl.pallas_call(
        tile_kernel,
        out_shape=jax.ShapeDtypeStruct((8, 256, 128), BF16),
        in_specs=[VMEM] * 17,
        out_specs=VMEM,
        scratch_shapes=[
            pltpu.VMEM((1280, 512), BF16),
            pltpu.VMEM((768, 512), BF16),
            pltpu.VMEM((256, 512), BF16),
            pltpu.VMEM((1536, 1024), BF16),
            pltpu.VMEM((1536, 256), BF16),
        ],
        cost_estimate=pl.CostEstimate(flops=1_500_000_000, bytes_accessed=8_000_000, transcendentals=0),
        compiler_params=pltpu.CompilerParams(vmem_limit_bytes=32 << 20),
        name="tile",
    )(*panels, *strips, cols)


def place_kernel(block_rows, own, other, *refs):
    outs, total = refs[:8], refs[8]
    group = lax.axis_index("grp")
    core = group & 1
    total[...] = jnp.zeros_like(total)
    for part in range(16):
        source, giver = (own, group) if part < 8 else (other, group ^ 1)
        target = block_rows[part % 8, giver]
        owner = target >> 1
        slot = (((owner >> 2) - (group >> 2)) & 3) * 4 + (((owner ^ group) >> 1) & 1) * 2 + (target & 1)

        @pl.when((owner & 1) == core)
        def _():
            total[slot] += source[part % 8].astype(F32)

    for dy in range(4):
        for half in range(2):
            outs[half * 4 + dy][...] = total[dy * 4 + half * 2 : dy * 4 + half * 2 + 2].astype(BF16)


def place(block_rows, own, other):
    return pl.pallas_call(
        place_kernel,
        out_shape=[jax.ShapeDtypeStruct((2, 256, 128), BF16)] * 8,
        in_specs=[SMEM, VMEM, VMEM],
        out_specs=[VMEM] * 8,
        scratch_shapes=[pltpu.VMEM((16, 256, 128), F32)],
        cost_estimate=pl.CostEstimate(flops=1_000_000, bytes_accessed=2_000_000, transcendentals=0),
        compiler_params=pltpu.CompilerParams(vmem_limit_bytes=32 << 20),
        name="place",
    )(block_rows, own, other)


def add_y(parts):
    moved = [part.astype(F32) for part in [parts[0]] + [hop_y(parts[dy], dy) for dy in (1, 2, 3)]]
    return (moved[0] + moved[2]) + (moved[1] + moved[3])


def step(panels, panel_owner, interface_cols, border, block_rows, pattern, block_x):
    strips = gather_blocks(border.T, "border")

    chunks = pack(panel_owner.T, panels)
    far = hop_x(chunks[2], 2)
    chunks = [chunks[0], hop_x(chunks[1], 1), far, hop_x(chunks[3], 3)]
    pieces = pick(panel_owner.T, chunks)
    pieces = [pieces[0]] + [hop_z(pieces[bits], bits) for bits in (1, 2, 3)]
    piece = pick_z(panel_owner.T, pieces)
    tile = make_tile(gather_blocks(piece, "panel"), strips, interface_cols)

    placed = place(block_rows.T, tile, swap_grp(tile, 1))
    other = add_y(placed[4:])
    mine = add_y(placed[:4])
    other = swap_grp(other.astype(BF16), 2)
    own_rows = (mine + other.astype(F32)).transpose(0, 2, 1)
    masked = own_rows.reshape(2, 128, 2, 128) * pattern.astype(F32)[:, None, :, None]
    schur = masked.reshape(256, 256).astype(BF16)

    partial = jnp.dot(schur, block_x, preferred_element_type=F32).astype(BF16)
    moved = [part.astype(F32) for part in [partial] + [hop_x(partial, dx) for dx in (1, 2, 3)]]
    row_sum = ((moved[0] + moved[2]) + (moved[1] + moved[3])).astype(BF16)
    moved = [part.astype(F32) for part in [row_sum] + [hop_z(row_sum, bits) for bits in (1, 2, 3)]]
    product = (moved[0] + moved[1]) + (moved[2] + moved[3])
    return (schur, product)


def solution(mesh):
    return jax.shard_map(
        step,
        mesh=mesh,
        in_specs=(
            P(("grp", "dev"), None, None),
            P(),
            P(None, ("grp", "dev")),
            P("grp", "dev"),
            P(),
            P("grp", "dev"),
            P("dev", None),
        ),
        out_specs=(P("grp", "dev"), P("grp", None)),
        check_vma=False,
    )
```

```python
import jax
import jax.numpy as jnp
from jax import lax
from jax.experimental import pallas as pl
from jax.experimental.pallas import tpu as pltpu
from jax.sharding import PartitionSpec as P


F32 = jnp.float32
BF16 = jnp.bfloat16
VMEM = pl.BlockSpec(memory_space=pltpu.VMEM)
SMEM = pl.BlockSpec(memory_space=pltpu.SMEM)


def hop_x(value, dx):
    perm = [(z * 4 + x, z * 4 + (x + dx) % 4) for z in range(4) for x in range(4)]
    return lax.ppermute(value, "dev", perm)


def hop_z(value, bits):
    perm = [(z * 4 + x, (z ^ bits) * 4 + x) for z in range(4) for x in range(4)]
    return lax.ppermute(value, "dev", perm)


def hop_y(value, dy):
    perm = [(y * 4 + r, ((y + dy) % 4) * 4 + r) for y in range(4) for r in range(4)]
    return lax.ppermute(value, "grp", perm)


def swap_grp(value, bits):
    return lax.ppermute(value, "grp", [(g, g ^ bits) for g in range(16)])


def pass_kernel(first, second, out_first, out_second):
    out_first[...] = first[...]
    out_second[...] = second[...]


def pass_on(first, second):
    return pl.pallas_call(
        pass_kernel,
        out_shape=[jax.ShapeDtypeStruct(value.shape, value.dtype) for value in (first, second)],
        in_specs=[VMEM] * 2,
        out_specs=[VMEM] * 2,
        cost_estimate=pl.CostEstimate(flops=1_000_000, bytes_accessed=1_600_000, transcendentals=0),
        compiler_params=pltpu.CompilerParams(vmem_limit_bytes=4 << 20),
        name="pass_on",
    )(first, second)


def gather_border(block):
    near = [hop_z(block, bits) for bits in (1, 2, 3)]
    low = jnp.stack([block, near[0]])
    high = jnp.stack([near[1], near[2]])
    low_left = hop_x(low, 1)
    high_right = hop_x(high, -1)
    high_left = hop_x(high, 1)
    low_right = hop_x(low, -1)
    sent_left, sent_right = pass_on(low_left, high_right)
    low_far = hop_x(sent_left, 1)
    high_far = hop_x(sent_right, -1)
    return [low, high, low_left, high_left, low_right, high_right, low_far, high_far]


def gather_panel(block):
    near = hop_z(block, 1)
    high = jnp.stack([hop_z(block, 2), hop_z(block, 3)])
    low = jnp.stack([block, near])
    low_left = hop_x(low, 1)
    low_right = hop_x(low, -1)
    high_right = hop_x(high, -1)
    high_left = hop_x(high, 1)
    low_far = hop_x(low_left, 1)
    high_far = hop_x(high_right, -1)
    return [low, high, low_left, high_left, low_right, high_right, low_far, high_far]


def block_source(part):
    dev = lax.axis_index("dev")
    return ((dev >> 2) ^ (part % 4)) * 4 + ((dev + (0, 3, 1, 2)[part // 4]) & 3)


HEIGHTS = (80, 48, 16)
OFFSETS = (0, 80, 128)
PIECE = 144


def pack_kernel(owners, slot, *refs):
    outs, held = refs[:4], refs[4]
    group, dev = lax.axis_index("grp"), lax.axis_index("dev")
    row = lax.broadcasted_iota(jnp.int32, (256, 256), 0)
    col = lax.broadcasted_iota(jnp.int32, (256, 256), 1)
    for step in range(3):

        @pl.when(owners[step, group] == dev)
        def _():
            top = 512 * step
            held[top + 256 :] = slot[0, top + 256 :]
            first = slot[0, top : top + 256, :256].astype(F32)
            second = slot[0, top + 256 : top + 512, 256:].astype(F32).T
            held[top + 256 : top + 512, 256:] = jnp.where(row > col, first, second).astype(BF16)
            height = HEIGHTS[step]
            for dx in range(4):
                for bits in range(4):
                    chunk = ((dev >> 2) ^ bits) * 4 + ((dev + dx) & 3)
                    start = pl.multiple_of(top + 256 + chunk * height, 16)
                    outs[dx][bits, :height] = held[pl.ds(start, height)]


def pack(owners, panels):
    return pl.pallas_call(
        pack_kernel,
        out_shape=[jax.ShapeDtypeStruct((4, HEIGHTS[0], 512), BF16)] * 4,
        in_specs=[SMEM, VMEM],
        out_specs=[VMEM] * 4,
        scratch_shapes=[pltpu.VMEM((1536, 512), BF16)],
        cost_estimate=pl.CostEstimate(flops=1_000_000, bytes_accessed=2_800_000, transcendentals=0),
        compiler_params=pltpu.CompilerParams(vmem_limit_bytes=16 << 20),
        name="pack",
    )(owners, panels)


def pick_kernel(owners, *refs):
    chunks, outs = refs[:4], refs[4:]
    group, dev = lax.axis_index("grp"), lax.axis_index("dev")
    for step in range(3):
        first, rows = OFFSETS[step], HEIGHTS[step]
        owner = owners[step, group]
        for dx in range(4):

            @pl.when(owner == (dev >> 2) * 4 + ((dev - dx) & 3))
            def _():
                for bits in range(4):
                    outs[bits][first : first + rows] = chunks[dx][bits, :rows]


def pick(owners, chunks):
    return pl.pallas_call(
        pick_kernel,
        out_shape=[jax.ShapeDtypeStruct((PIECE, 512), BF16)] * 4,
        in_specs=[SMEM] + [VMEM] * 4,
        out_specs=[VMEM] * 4,
        cost_estimate=pl.CostEstimate(flops=1_000_000, bytes_accessed=1_200_000, transcendentals=0),
        compiler_params=pltpu.CompilerParams(vmem_limit_bytes=8 << 20),
        name="pick",
    )(owners, *chunks)


def pick_z_kernel(owners, *refs):
    pieces, out = refs[:4], refs[4]
    group, dev = lax.axis_index("grp"), lax.axis_index("dev")
    for step in range(3):
        first, rows = OFFSETS[step], HEIGHTS[step]
        distance = (owners[step, group] ^ dev) >> 2
        for bits in range(4):

            @pl.when(distance == bits)
            def _():
                out[first : first + rows] = pieces[bits][first : first + rows]


def pick_z(owners, pieces):
    return pl.pallas_call(
        pick_z_kernel,
        out_shape=jax.ShapeDtypeStruct((PIECE, 512), BF16),
        in_specs=[SMEM] + [VMEM] * 4,
        out_specs=VMEM,
        cost_estimate=pl.CostEstimate(flops=1_000_000, bytes_accessed=300_000, transcendentals=0),
        compiler_params=pltpu.CompilerParams(vmem_limit_bytes=4 << 20),
        name="pick_z",
    )(owners, *pieces)


def tile_kernel(*refs):
    panels, strips, (cols, out, pan0, pan1, pan2, border, answer) = refs[:8], refs[8:16], refs[16:]
    half = 256
    pans = (pan0, pan1, pan2)
    sources = [block_source(part) for part in range(16)]
    row = lax.broadcasted_iota(jnp.int32, (half, half), 0)
    col = lax.broadcasted_iota(jnp.int32, (half, half), 1)

    def dot(a, b):
        return jnp.dot(a, b, preferred_element_type=F32)

    def unit(below):
        return jnp.where(row > col, below, jnp.where(row == col, 1.0, 0.0)).astype(BF16)

    def inverse_times(step, current):
        pan, first, rows = pans[step], OFFSETS[step], HEIGHTS[step]
        for part, source in enumerate(sources):
            pan[pl.ds(pl.multiple_of(source * rows, 16), rows)] = panels[part // 2][part % 2, first : first + rows]
        shared = pan[:half, half:].astype(F32)
        high, low = current[:half], current[half:]
        upper = dot(unit(shared), high)
        lower = dot(pan[:half, :half], high) + dot(unit(shared.T), low)
        result = jnp.concatenate([upper, lower], axis=0).astype(BF16)
        answer[step * 512 : step * 512 + 512] = result
        return result

    first = inverse_times(0, cols[:512])
    rest = cols[512:].astype(F32) - dot(pan0[half:], first)
    second = inverse_times(1, rest[:512].astype(BF16))
    rest = rest[512:] - dot(pan1[half:], second)
    inverse_times(2, rest.astype(BF16))
    for part, source in enumerate(sources):
        border[pl.ds(pl.multiple_of(source * 96, 32), 96)] = strips[part // 2][part % 2]
    tile = lax.dot_general(answer[...], border[...], (((0,), (0,)), ((), ())), preferred_element_type=F32)
    for block in range(8):
        out[block] = tile[:, block * 128 : block * 128 + 128].astype(BF16)


def make_tile(panels, strips, cols):
    return pl.pallas_call(
        tile_kernel,
        out_shape=jax.ShapeDtypeStruct((8, 256, 128), BF16),
        in_specs=[VMEM] * 17,
        out_specs=VMEM,
        scratch_shapes=[
            pltpu.VMEM((1280, 512), BF16),
            pltpu.VMEM((768, 512), BF16),
            pltpu.VMEM((256, 512), BF16),
            pltpu.VMEM((1536, 1024), BF16),
            pltpu.VMEM((1536, 256), BF16),
        ],
        cost_estimate=pl.CostEstimate(flops=1_500_000_000, bytes_accessed=8_000_000, transcendentals=0),
        compiler_params=pltpu.CompilerParams(vmem_limit_bytes=32 << 20),
        name="tile",
    )(*panels, *strips, cols)


def place_kernel(block_rows, own, other, *refs):
    outs, total = refs[:8], refs[8]
    group = lax.axis_index("grp")
    core = group & 1
    total[...] = jnp.zeros_like(total)
    for part in range(16):
        source, giver = (own, group) if part < 8 else (other, group ^ 1)
        target = block_rows[part % 8, giver]
        owner = target >> 1
        slot = (((owner >> 2) - (group >> 2)) & 3) * 4 + (((owner ^ group) >> 1) & 1) * 2 + (target & 1)

        @pl.when((owner & 1) == core)
        def _():
            total[slot] += source[part % 8].astype(F32)

    for dy in range(4):
        for half in range(2):
            outs[half * 4 + dy][...] = total[dy * 4 + half * 2 : dy * 4 + half * 2 + 2].astype(BF16)


def place(block_rows, own, other):
    return pl.pallas_call(
        place_kernel,
        out_shape=[jax.ShapeDtypeStruct((2, 256, 128), BF16)] * 8,
        in_specs=[SMEM, VMEM, VMEM],
        out_specs=[VMEM] * 8,
        scratch_shapes=[pltpu.VMEM((16, 256, 128), F32)],
        cost_estimate=pl.CostEstimate(flops=1_000_000, bytes_accessed=2_000_000, transcendentals=0),
        compiler_params=pltpu.CompilerParams(vmem_limit_bytes=32 << 20),
        name="place",
    )(block_rows, own, other)


def add_y(parts):
    moved = [part.astype(F32) for part in [parts[0]] + [hop_y(parts[dy], dy) for dy in (1, 2, 3)]]
    return (moved[0] + moved[2]) + (moved[1] + moved[3])


def step(panels, panel_owner, interface_cols, border, block_rows, pattern, block_x):
    strips = gather_border(border.T)

    chunks = pack(panel_owner.T, panels)
    far = hop_x(chunks[2], 2)
    chunks = [chunks[0], hop_x(chunks[1], 1), far, hop_x(chunks[3], 3)]
    pieces = pick(panel_owner.T, chunks)
    pieces = [pieces[0]] + [hop_z(pieces[bits], bits) for bits in (1, 2, 3)]
    piece = pick_z(panel_owner.T, pieces)
    tile = make_tile(gather_panel(piece), strips, interface_cols)

    placed = place(block_rows.T, tile, swap_grp(tile, 1))
    other = add_y(placed[4:])
    mine = add_y(placed[:4])
    other = swap_grp(other.astype(BF16), 2)
    own_rows = (mine + other.astype(F32)).transpose(0, 2, 1)
    masked = own_rows.reshape(2, 128, 2, 128) * pattern.astype(F32)[:, None, :, None]
    schur = masked.reshape(256, 256).astype(BF16)

    partial = jnp.dot(schur, block_x, preferred_element_type=F32).astype(BF16)
    moved = [part.astype(F32) for part in [partial] + [hop_x(partial, dx) for dx in (1, 2, 3)]]
    row_sum = ((moved[0] + moved[2]) + (moved[1] + moved[3])).astype(BF16)
    moved = [part.astype(F32) for part in [row_sum] + [hop_z(row_sum, bits) for bits in (1, 2, 3)]]
    product = (moved[0] + moved[1]) + (moved[2] + moved[3])
    return (schur, product)


def solution(mesh):
    return jax.shard_map(
        step,
        mesh=mesh,
        in_specs=(
            P(("grp", "dev"), None, None),
            P(),
            P(None, ("grp", "dev")),
            P("grp", "dev"),
            P(),
            P("grp", "dev"),
            P("dev", None),
        ),
        out_specs=(P("grp", "dev"), P("grp", None)),
        check_vma=False,
    )
```

```python
import jax
import jax.numpy as jnp
from jax import lax
from jax.experimental import pallas as pl
from jax.experimental.pallas import tpu as pltpu
from jax.sharding import PartitionSpec as P


F32 = jnp.float32
BF16 = jnp.bfloat16
VMEM = pl.BlockSpec(memory_space=pltpu.VMEM)
SMEM = pl.BlockSpec(memory_space=pltpu.SMEM)


def hop_x(value, dx):
    perm = [(z * 4 + x, z * 4 + (x + dx) % 4) for z in range(4) for x in range(4)]
    return lax.ppermute(value, "dev", perm)


def hop_z(value, bits):
    perm = [(z * 4 + x, (z ^ bits) * 4 + x) for z in range(4) for x in range(4)]
    return lax.ppermute(value, "dev", perm)


def hop_y(value, dy):
    perm = [(y * 4 + r, ((y + dy) % 4) * 4 + r) for y in range(4) for r in range(4)]
    return lax.ppermute(value, "grp", perm)


def swap_grp(value, bits):
    return lax.ppermute(value, "grp", [(g, g ^ bits) for g in range(16)])


def pass_kernel(first, second, out_first, out_second):
    out_first[...] = first[...]
    out_second[...] = second[...]


def pass_on(first, second):
    return pl.pallas_call(
        pass_kernel,
        out_shape=[jax.ShapeDtypeStruct(value.shape, value.dtype) for value in (first, second)],
        in_specs=[VMEM] * 2,
        out_specs=[VMEM] * 2,
        cost_estimate=pl.CostEstimate(flops=1_000_000, bytes_accessed=1_600_000, transcendentals=0),
        compiler_params=pltpu.CompilerParams(vmem_limit_bytes=4 << 20),
        name="pass_on",
    )(first, second)


def gather_border(block):
    near = [hop_z(block, bits) for bits in (1, 2, 3)]
    low = jnp.stack([block, near[0]])
    high = jnp.stack([near[1], near[2]])
    low_left = hop_x(low, 1)
    high_right = hop_x(high, -1)
    high_left = hop_x(high, 1)
    low_right = hop_x(low, -1)
    sent_left, sent_right = pass_on(low_left, high_right)
    low_far = hop_x(sent_left, 1)
    high_far = hop_x(sent_right, -1)
    return [low, high, low_left, high_left, low_right, high_right, low_far, high_far]


def gather_panel(block):
    near = hop_z(block, 1)
    high = jnp.stack([hop_z(block, 2), hop_z(block, 3)])
    low = jnp.stack([block, near])
    low_left = hop_x(low, 1)
    low_right = hop_x(low, -1)
    high_right = hop_x(high, -1)
    high_left = hop_x(high, 1)
    low_far = hop_x(low_left, 1)
    high_far = hop_x(high_right, -1)
    return [low, high, low_left, high_left, low_right, high_right, low_far, high_far]


def block_source(part):
    dev = lax.axis_index("dev")
    return ((dev >> 2) ^ (part % 4)) * 4 + ((dev + (0, 3, 1, 2)[part // 4]) & 3)


HEIGHTS = (80, 48, 16)
OFFSETS = (0, 80, 128)
PIECE = 144


def early_kernel(out):
    out[...] = jnp.zeros_like(out)


def early():
    return pl.pallas_call(
        early_kernel,
        out_shape=jax.ShapeDtypeStruct((8, 128), F32),
        out_specs=VMEM,
        cost_estimate=pl.CostEstimate(flops=4_000_000_000, bytes_accessed=4096, transcendentals=0),
        compiler_params=pltpu.CompilerParams(vmem_limit_bytes=1 << 20),
        name="early",
    )()


def pack_kernel(owners, slot, unused, *refs):
    outs, held = refs[:4], refs[4]
    group, dev = lax.axis_index("grp"), lax.axis_index("dev")
    row = lax.broadcasted_iota(jnp.int32, (256, 256), 0)
    col = lax.broadcasted_iota(jnp.int32, (256, 256), 1)
    for step in range(3):

        @pl.when(owners[step, group] == dev)
        def _():
            top = 512 * step
            held[top + 256 :] = slot[0, top + 256 :]
            first = slot[0, top : top + 256, :256].astype(F32)
            second = slot[0, top + 256 : top + 512, 256:].astype(F32).T
            held[top + 256 : top + 512, 256:] = jnp.where(row > col, first, second).astype(BF16)
            height = HEIGHTS[step]
            for dx in range(4):
                for bits in range(4):
                    chunk = ((dev >> 2) ^ bits) * 4 + ((dev + dx) & 3)
                    start = pl.multiple_of(top + 256 + chunk * height, 16)
                    outs[dx][bits, :height] = held[pl.ds(start, height)]


def pack(owners, panels, first):
    return pl.pallas_call(
        pack_kernel,
        out_shape=[jax.ShapeDtypeStruct((4, HEIGHTS[0], 512), BF16)] * 4,
        in_specs=[SMEM, VMEM, VMEM],
        out_specs=[VMEM] * 4,
        scratch_shapes=[pltpu.VMEM((1536, 512), BF16)],
        cost_estimate=pl.CostEstimate(flops=1_000_000, bytes_accessed=2_800_000, transcendentals=0),
        compiler_params=pltpu.CompilerParams(vmem_limit_bytes=16 << 20),
        name="pack",
    )(owners, panels, first)


def pick_kernel(owners, *refs):
    chunks, outs = refs[:4], refs[4:]
    group, dev = lax.axis_index("grp"), lax.axis_index("dev")
    for step in range(3):
        first, rows = OFFSETS[step], HEIGHTS[step]
        owner = owners[step, group]
        for dx in range(4):

            @pl.when(owner == (dev >> 2) * 4 + ((dev - dx) & 3))
            def _():
                for bits in range(4):
                    outs[bits][first : first + rows] = chunks[dx][bits, :rows]


def pick(owners, chunks):
    return pl.pallas_call(
        pick_kernel,
        out_shape=[jax.ShapeDtypeStruct((PIECE, 512), BF16)] * 4,
        in_specs=[SMEM] + [VMEM] * 4,
        out_specs=[VMEM] * 4,
        cost_estimate=pl.CostEstimate(flops=1_000_000, bytes_accessed=1_200_000, transcendentals=0),
        compiler_params=pltpu.CompilerParams(vmem_limit_bytes=8 << 20),
        name="pick",
    )(owners, *chunks)


def pick_z_kernel(owners, *refs):
    pieces, out = refs[:4], refs[4]
    group, dev = lax.axis_index("grp"), lax.axis_index("dev")
    for step in range(3):
        first, rows = OFFSETS[step], HEIGHTS[step]
        distance = (owners[step, group] ^ dev) >> 2
        for bits in range(4):

            @pl.when(distance == bits)
            def _():
                out[first : first + rows] = pieces[bits][first : first + rows]


def pick_z(owners, pieces):
    return pl.pallas_call(
        pick_z_kernel,
        out_shape=jax.ShapeDtypeStruct((PIECE, 512), BF16),
        in_specs=[SMEM] + [VMEM] * 4,
        out_specs=VMEM,
        cost_estimate=pl.CostEstimate(flops=1_000_000, bytes_accessed=300_000, transcendentals=0),
        compiler_params=pltpu.CompilerParams(vmem_limit_bytes=4 << 20),
        name="pick_z",
    )(owners, *pieces)


def tile_kernel(*refs):
    panels, strips, (cols, out, pan0, pan1, pan2, border, answer) = refs[:8], refs[8:16], refs[16:]
    half = 256
    pans = (pan0, pan1, pan2)
    sources = [block_source(part) for part in range(16)]
    row = lax.broadcasted_iota(jnp.int32, (half, half), 0)
    col = lax.broadcasted_iota(jnp.int32, (half, half), 1)

    def dot(a, b):
        return jnp.dot(a, b, preferred_element_type=F32)

    def unit(below):
        return jnp.where(row > col, below, jnp.where(row == col, 1.0, 0.0)).astype(BF16)

    def inverse_times(step, current):
        pan, first, rows = pans[step], OFFSETS[step], HEIGHTS[step]
        for part, source in enumerate(sources):
            pan[pl.ds(pl.multiple_of(source * rows, 16), rows)] = panels[part // 2][part % 2, first : first + rows]
        shared = pan[:half, half:].astype(F32)
        high, low = current[:half], current[half:]
        upper = dot(unit(shared), high)
        lower = dot(pan[:half, :half], high) + dot(unit(shared.T), low)
        result = jnp.concatenate([upper, lower], axis=0).astype(BF16)
        answer[step * 512 : step * 512 + 512] = result
        return result

    first = inverse_times(0, cols[:512])
    rest = cols[512:].astype(F32) - dot(pan0[half:], first)
    second = inverse_times(1, rest[:512].astype(BF16))
    rest = rest[512:] - dot(pan1[half:], second)
    inverse_times(2, rest.astype(BF16))
    for part, source in enumerate(sources):
        border[pl.ds(pl.multiple_of(source * 96, 32), 96)] = strips[part // 2][part % 2]
    tile = lax.dot_general(answer[...], border[...], (((0,), (0,)), ((), ())), preferred_element_type=F32)
    for block in range(8):
        out[block] = tile[:, block * 128 : block * 128 + 128].astype(BF16)


def make_tile(panels, strips, cols):
    return pl.pallas_call(
        tile_kernel,
        out_shape=jax.ShapeDtypeStruct((8, 256, 128), BF16),
        in_specs=[VMEM] * 17,
        out_specs=VMEM,
        scratch_shapes=[
            pltpu.VMEM((1280, 512), BF16),
            pltpu.VMEM((768, 512), BF16),
            pltpu.VMEM((256, 512), BF16),
            pltpu.VMEM((1536, 1024), BF16),
            pltpu.VMEM((1536, 256), BF16),
        ],
        cost_estimate=pl.CostEstimate(flops=1_500_000_000, bytes_accessed=8_000_000, transcendentals=0),
        compiler_params=pltpu.CompilerParams(vmem_limit_bytes=32 << 20),
        name="tile",
    )(*panels, *strips, cols)


def place_kernel(block_rows, own, other, *refs):
    outs, total = refs[:8], refs[8]
    group = lax.axis_index("grp")
    core = group & 1
    total[...] = jnp.zeros_like(total)
    for part in range(16):
        source, giver = (own, group) if part < 8 else (other, group ^ 1)
        target = block_rows[part % 8, giver]
        owner = target >> 1
        slot = (((owner >> 2) - (group >> 2)) & 3) * 4 + (((owner ^ group) >> 1) & 1) * 2 + (target & 1)

        @pl.when((owner & 1) == core)
        def _():
            total[slot] += source[part % 8].astype(F32)

    for dy in range(4):
        for half in range(2):
            outs[half * 4 + dy][...] = total[dy * 4 + half * 2 : dy * 4 + half * 2 + 2].astype(BF16)


def place(block_rows, own, other):
    return pl.pallas_call(
        place_kernel,
        out_shape=[jax.ShapeDtypeStruct((2, 256, 128), BF16)] * 8,
        in_specs=[SMEM, VMEM, VMEM],
        out_specs=[VMEM] * 8,
        scratch_shapes=[pltpu.VMEM((16, 256, 128), F32)],
        cost_estimate=pl.CostEstimate(flops=1_000_000, bytes_accessed=2_000_000, transcendentals=0),
        compiler_params=pltpu.CompilerParams(vmem_limit_bytes=32 << 20),
        name="place",
    )(block_rows, own, other)


def add_y(parts):
    moved = [part.astype(F32) for part in [parts[0]] + [hop_y(parts[dy], dy) for dy in (1, 2, 3)]]
    return (moved[0] + moved[2]) + (moved[1] + moved[3])


def step(panels, panel_owner, interface_cols, border, block_rows, pattern, block_x):
    strips = gather_border(border.T)

    chunks = pack(panel_owner.T, panels, early())
    far = hop_x(chunks[2], 2)
    chunks = [chunks[0], hop_x(chunks[1], 1), far, hop_x(chunks[3], 3)]
    pieces = pick(panel_owner.T, chunks)
    pieces = [pieces[0]] + [hop_z(pieces[bits], bits) for bits in (1, 2, 3)]
    piece = pick_z(panel_owner.T, pieces)
    tile = make_tile(gather_panel(piece), strips, interface_cols)

    placed = place(block_rows.T, tile, swap_grp(tile, 1))
    other = add_y(placed[4:])
    mine = add_y(placed[:4])
    other = swap_grp(other.astype(BF16), 2)
    own_rows = (mine + other.astype(F32)).transpose(0, 2, 1)
    masked = own_rows.reshape(2, 128, 2, 128) * pattern.astype(F32)[:, None, :, None]
    schur = masked.reshape(256, 256).astype(BF16)

    partial = jnp.dot(schur, block_x, preferred_element_type=F32).astype(BF16)
    moved = [part.astype(F32) for part in [partial] + [hop_x(partial, dx) for dx in (1, 2, 3)]]
    row_sum = ((moved[0] + moved[2]) + (moved[1] + moved[3])).astype(BF16)
    moved = [part.astype(F32) for part in [row_sum] + [hop_z(row_sum, bits) for bits in (1, 2, 3)]]
    product = (moved[0] + moved[1]) + (moved[2] + moved[3])
    return (schur, product)


def solution(mesh):
    return jax.shard_map(
        step,
        mesh=mesh,
        in_specs=(
            P(("grp", "dev"), None, None),
            P(),
            P(None, ("grp", "dev")),
            P("grp", "dev"),
            P(),
            P("grp", "dev"),
            P("dev", None),
        ),
        out_specs=(P("grp", "dev"), P("grp", None)),
        check_vma=False,
    )
```

```python
import jax
import jax.numpy as jnp
from jax import lax
from jax.experimental import pallas as pl
from jax.experimental.pallas import tpu as pltpu
from jax.sharding import PartitionSpec as P


F32 = jnp.float32
BF16 = jnp.bfloat16
VMEM = pl.BlockSpec(memory_space=pltpu.VMEM)
SMEM = pl.BlockSpec(memory_space=pltpu.SMEM)


def hop_x(value, dx):
    perm = [(z * 4 + x, z * 4 + (x + dx) % 4) for z in range(4) for x in range(4)]
    return lax.ppermute(value, "dev", perm)


def hop_z(value, bits):
    perm = [(z * 4 + x, (z ^ bits) * 4 + x) for z in range(4) for x in range(4)]
    return lax.ppermute(value, "dev", perm)


def hops_z(values):
    out = []
    for bits, value in zip((1, 2, 3), values):
        out.append(hop_z(value, bits))
    return out


def hop_y(value, dy):
    perm = [(y * 4 + r, ((y + dy) % 4) * 4 + r) for y in range(4) for r in range(4)]
    return lax.ppermute(value, "grp", perm)


def swap_grp(value, bits):
    return lax.ppermute(value, "grp", [(g, g ^ bits) for g in range(16)])


def pass_kernel(first, second, out_first, out_second):
    out_first[...] = first[...]
    out_second[...] = second[...]


def pass_on(first, second):
    return pl.pallas_call(
        pass_kernel,
        out_shape=[jax.ShapeDtypeStruct(value.shape, value.dtype) for value in (first, second)],
        in_specs=[VMEM] * 2,
        out_specs=[VMEM] * 2,
        cost_estimate=pl.CostEstimate(flops=1_000_000, bytes_accessed=1_600_000, transcendentals=0),
        compiler_params=pltpu.CompilerParams(vmem_limit_bytes=4 << 20),
        name="pass_on",
    )(first, second)


def gather_border(block):
    near = [hop_z(block, bits) for bits in (1, 2, 3)]
    low = jnp.stack([block, near[0]])
    high = jnp.stack([near[1], near[2]])
    low_left = hop_x(low, 1)
    high_right = hop_x(high, -1)
    high_left = hop_x(high, 1)
    low_right = hop_x(low, -1)
    sent_left, sent_right = pass_on(low_left, high_right)
    low_far = hop_x(sent_left, 1)
    high_far = hop_x(sent_right, -1)
    return [low, high, low_left, high_left, low_right, high_right, low_far, high_far]


def gather_panel(block):
    near = hop_z(block, 1)
    high = jnp.stack([hop_z(block, 2), hop_z(block, 3)])
    low = jnp.stack([block, near])
    low_left = hop_x(low, 1)
    low_right = hop_x(low, -1)
    high_right = hop_x(high, -1)
    high_left = hop_x(high, 1)
    low_far = hop_x(low_left, 1)
    high_far = hop_x(high_right, -1)
    return [low, high, low_left, high_left, low_right, high_right, low_far, high_far]


def block_source(part):
    dev = lax.axis_index("dev")
    return ((dev >> 2) ^ (part % 4)) * 4 + ((dev + (0, 3, 1, 2)[part // 4]) & 3)


HEIGHTS = (80, 48, 16)
OFFSETS = (0, 80, 128)
PIECE = 144


def early_kernel(out):
    out[...] = jnp.zeros_like(out)


def early():
    return pl.pallas_call(
        early_kernel,
        out_shape=jax.ShapeDtypeStruct((8, 128), F32),
        out_specs=VMEM,
        cost_estimate=pl.CostEstimate(flops=4_000_000_000, bytes_accessed=4096, transcendentals=0),
        compiler_params=pltpu.CompilerParams(vmem_limit_bytes=1 << 20),
        name="early",
    )()


def pack_kernel(owners, slot, unused, *refs):
    outs, held = refs[:4], refs[4]
    group, dev = lax.axis_index("grp"), lax.axis_index("dev")
    row = lax.broadcasted_iota(jnp.int32, (256, 256), 0)
    col = lax.broadcasted_iota(jnp.int32, (256, 256), 1)
    for step in range(3):

        @pl.when(owners[step, group] == dev)
        def _():
            top = 512 * step
            held[top + 256 :] = slot[0, top + 256 :]
            first = slot[0, top : top + 256, :256].astype(F32)
            second = slot[0, top + 256 : top + 512, 256:].astype(F32).T
            held[top + 256 : top + 512, 256:] = jnp.where(row > col, first, second).astype(BF16)
            height = HEIGHTS[step]
            for dx in range(4):
                for bits in range(4):
                    chunk = ((dev >> 2) ^ bits) * 4 + ((dev + dx) & 3)
                    start = pl.multiple_of(top + 256 + chunk * height, 16)
                    outs[dx][bits, :height] = held[pl.ds(start, height)]


def pack(owners, panels, first):
    return pl.pallas_call(
        pack_kernel,
        out_shape=[jax.ShapeDtypeStruct((4, HEIGHTS[0], 512), BF16)] * 4,
        in_specs=[SMEM, VMEM, VMEM],
        out_specs=[VMEM] * 4,
        scratch_shapes=[pltpu.VMEM((1536, 512), BF16)],
        cost_estimate=pl.CostEstimate(flops=1_000_000, bytes_accessed=2_800_000, transcendentals=0),
        compiler_params=pltpu.CompilerParams(vmem_limit_bytes=16 << 20),
        name="pack",
    )(owners, panels, first)


def pick_kernel(owners, *refs):
    chunks, outs = refs[:4], refs[4:]
    group, dev = lax.axis_index("grp"), lax.axis_index("dev")
    for step in range(3):
        first, rows = OFFSETS[step], HEIGHTS[step]
        owner = owners[step, group]
        for dx in range(4):

            @pl.when(owner == (dev >> 2) * 4 + ((dev - dx) & 3))
            def _():
                for bits in range(4):
                    outs[bits][first : first + rows] = chunks[dx][bits, :rows]


def pick(owners, chunks):
    return pl.pallas_call(
        pick_kernel,
        out_shape=[jax.ShapeDtypeStruct((PIECE, 512), BF16)] * 4,
        in_specs=[SMEM] + [VMEM] * 4,
        out_specs=[VMEM] * 4,
        cost_estimate=pl.CostEstimate(flops=1_000_000, bytes_accessed=1_200_000, transcendentals=0),
        compiler_params=pltpu.CompilerParams(vmem_limit_bytes=8 << 20),
        name="pick",
    )(owners, *chunks)


def pick_z_kernel(owners, *refs):
    pieces, out = refs[:4], refs[4]
    group, dev = lax.axis_index("grp"), lax.axis_index("dev")
    for step in range(3):
        first, rows = OFFSETS[step], HEIGHTS[step]
        distance = (owners[step, group] ^ dev) >> 2
        for bits in range(4):

            @pl.when(distance == bits)
            def _():
                out[first : first + rows] = pieces[bits][first : first + rows]


def pick_z(owners, pieces):
    return pl.pallas_call(
        pick_z_kernel,
        out_shape=jax.ShapeDtypeStruct((PIECE, 512), BF16),
        in_specs=[SMEM] + [VMEM] * 4,
        out_specs=VMEM,
        cost_estimate=pl.CostEstimate(flops=1_000_000, bytes_accessed=300_000, transcendentals=0),
        compiler_params=pltpu.CompilerParams(vmem_limit_bytes=4 << 20),
        name="pick_z",
    )(owners, *pieces)


def tile_kernel(*refs):
    panels, strips, (cols, out, pan0, pan1, pan2, border, answer) = refs[:8], refs[8:16], refs[16:]
    half = 256
    pans = (pan0, pan1, pan2)
    sources = [block_source(part) for part in range(16)]
    row = lax.broadcasted_iota(jnp.int32, (half, half), 0)
    col = lax.broadcasted_iota(jnp.int32, (half, half), 1)

    def dot(a, b):
        return jnp.dot(a, b, preferred_element_type=F32)

    def unit(below):
        return jnp.where(row > col, below, jnp.where(row == col, 1.0, 0.0)).astype(BF16)

    def inverse_times(step, current):
        pan, first, rows = pans[step], OFFSETS[step], HEIGHTS[step]
        for part, source in enumerate(sources):
            pan[pl.ds(pl.multiple_of(source * rows, 16), rows)] = panels[part // 2][part % 2, first : first + rows]
        shared = pan[:half, half:].astype(F32)
        high, low = current[:half], current[half:]
        upper = dot(unit(shared), high)
        lower = dot(pan[:half, :half], high) + dot(unit(shared.T), low)
        result = jnp.concatenate([upper, lower], axis=0).astype(BF16)
        answer[step * 512 : step * 512 + 512] = result
        return result

    first = inverse_times(0, cols[:512])
    rest = cols[512:].astype(F32) - dot(pan0[half:], first)
    second = inverse_times(1, rest[:512].astype(BF16))
    rest = rest[512:] - dot(pan1[half:], second)
    inverse_times(2, rest.astype(BF16))
    for part, source in enumerate(sources):
        border[pl.ds(pl.multiple_of(source * 96, 32), 96)] = strips[part // 2][part % 2]
    tile = lax.dot_general(answer[...], border[...], (((0,), (0,)), ((), ())), preferred_element_type=F32)
    for block in range(8):
        out[block] = tile[:, block * 128 : block * 128 + 128].astype(BF16)


def make_tile(panels, strips, cols):
    return pl.pallas_call(
        tile_kernel,
        out_shape=jax.ShapeDtypeStruct((8, 256, 128), BF16),
        in_specs=[VMEM] * 17,
        out_specs=VMEM,
        scratch_shapes=[
            pltpu.VMEM((1280, 512), BF16),
            pltpu.VMEM((768, 512), BF16),
            pltpu.VMEM((256, 512), BF16),
            pltpu.VMEM((1536, 1024), BF16),
            pltpu.VMEM((1536, 256), BF16),
        ],
        cost_estimate=pl.CostEstimate(flops=1_500_000_000, bytes_accessed=8_000_000, transcendentals=0),
        compiler_params=pltpu.CompilerParams(vmem_limit_bytes=32 << 20),
        name="tile",
    )(*panels, *strips, cols)


def place_kernel(block_rows, own, other, *refs):
    outs, total = refs[:8], refs[8]
    group = lax.axis_index("grp")
    core = group & 1
    total[...] = jnp.zeros_like(total)
    for part in range(16):
        source, giver = (own, group) if part < 8 else (other, group ^ 1)
        target = block_rows[part % 8, giver]
        owner = target >> 1
        slot = (((owner >> 2) - (group >> 2)) & 3) * 4 + (((owner ^ group) >> 1) & 1) * 2 + (target & 1)

        @pl.when((owner & 1) == core)
        def _():
            total[slot] += source[part % 8].astype(F32)

    for dy in range(4):
        for half in range(2):
            outs[half * 4 + dy][...] = total[dy * 4 + half * 2 : dy * 4 + half * 2 + 2].astype(BF16)


def place(block_rows, own, other):
    return pl.pallas_call(
        place_kernel,
        out_shape=[jax.ShapeDtypeStruct((2, 256, 128), BF16)] * 8,
        in_specs=[SMEM, VMEM, VMEM],
        out_specs=[VMEM] * 8,
        scratch_shapes=[pltpu.VMEM((16, 256, 128), F32)],
        cost_estimate=pl.CostEstimate(flops=1_000_000, bytes_accessed=2_000_000, transcendentals=0),
        compiler_params=pltpu.CompilerParams(vmem_limit_bytes=32 << 20),
        name="place",
    )(block_rows, own, other)


def add_y(parts):
    moved = [part.astype(F32) for part in [parts[0]] + [hop_y(parts[dy], dy) for dy in (1, 2, 3)]]
    return (moved[0] + moved[2]) + (moved[1] + moved[3])


def step(panels, panel_owner, interface_cols, border, block_rows, pattern, block_x):
    strips = gather_border(border.T)

    chunks = pack(panel_owner.T, panels, early())
    far = hop_x(chunks[2], 2)
    chunks = [chunks[0], hop_x(chunks[1], 1), far, hop_x(chunks[3], 3)]
    pieces = pick(panel_owner.T, chunks)
    pieces = [pieces[0]] + hops_z(pieces[1:])
    piece = pick_z(panel_owner.T, pieces)
    tile = make_tile(gather_panel(piece), strips, interface_cols)

    placed = place(block_rows.T, tile, swap_grp(tile, 1))
    other = add_y(placed[4:])
    mine = add_y(placed[:4])
    other = swap_grp(other.astype(BF16), 2)
    own_rows = (mine + other.astype(F32)).transpose(0, 2, 1)
    masked = own_rows.reshape(2, 128, 2, 128) * pattern.astype(F32)[:, None, :, None]
    schur = masked.reshape(256, 256).astype(BF16)

    partial = jnp.dot(schur, block_x, preferred_element_type=F32).astype(BF16)
    moved = [part.astype(F32) for part in [partial] + [hop_x(partial, dx) for dx in (1, 2, 3)]]
    row_sum = ((moved[0] + moved[2]) + (moved[1] + moved[3])).astype(BF16)
    moved = [part.astype(F32) for part in [row_sum] + hops_z([row_sum] * 3)]
    product = (moved[0] + moved[1]) + (moved[2] + moved[3])
    return (schur, product)


def solution(mesh):
    return jax.shard_map(
        step,
        mesh=mesh,
        in_specs=(
            P(("grp", "dev"), None, None),
            P(),
            P(None, ("grp", "dev")),
            P("grp", "dev"),
            P(),
            P("grp", "dev"),
            P("dev", None),
        ),
        out_specs=(P("grp", "dev"), P("grp", None)),
        check_vma=False,
    )
```

```python
import jax
import jax.numpy as jnp
from jax import lax
from jax.experimental import pallas as pl
from jax.experimental.pallas import tpu as pltpu
from jax.sharding import PartitionSpec as P


F32 = jnp.float32
BF16 = jnp.bfloat16
VMEM = pl.BlockSpec(memory_space=pltpu.VMEM)
SMEM = pl.BlockSpec(memory_space=pltpu.SMEM)


def hop_x(value, dx):
    perm = [(z * 4 + x, z * 4 + (x + dx) % 4) for z in range(4) for x in range(4)]
    return lax.ppermute(value, "dev", perm)


def hop_z(value, bits):
    perm = [(z * 4 + x, (z ^ bits) * 4 + x) for z in range(4) for x in range(4)]
    return lax.ppermute(value, "dev", perm)


def hops_z(values):
    out = []
    for bits, value in zip((1, 2, 3), values):
        out.append(hop_z(value, bits))
    return out


def hop_y(value, dy):
    perm = [(y * 4 + r, ((y + dy) % 4) * 4 + r) for y in range(4) for r in range(4)]
    return lax.ppermute(value, "grp", perm)


def swap_grp(value, bits):
    return lax.ppermute(value, "grp", [(g, g ^ bits) for g in range(16)])


def pass_kernel(first, second, out_first, out_second):
    out_first[...] = first[...]
    out_second[...] = second[...]


def pass_on(first, second):
    return pl.pallas_call(
        pass_kernel,
        out_shape=[jax.ShapeDtypeStruct(value.shape, value.dtype) for value in (first, second)],
        in_specs=[VMEM] * 2,
        out_specs=[VMEM] * 2,
        cost_estimate=pl.CostEstimate(flops=1_000_000, bytes_accessed=1_600_000, transcendentals=0),
        compiler_params=pltpu.CompilerParams(vmem_limit_bytes=4 << 20),
        name="pass_on",
    )(first, second)


def gather_border(block):
    near = [hop_z(block, bits) for bits in (1, 2, 3)]
    low = jnp.stack([block, near[0]])
    high = jnp.stack([near[1], near[2]])
    low_left = hop_x(low, 1)
    high_right = hop_x(high, -1)
    high_left = hop_x(high, 1)
    low_right = hop_x(low, -1)
    sent_left, sent_right = pass_on(low_left, high_right)
    low_far = hop_x(sent_left, 1)
    high_far = hop_x(sent_right, -1)
    return [low, high, low_left, high_left, low_right, high_right, low_far, high_far]


def gather_panel(block):
    near = hop_z(block, 1)
    high = jnp.stack([hop_z(block, 2), hop_z(block, 3)])
    low = jnp.stack([block, near])
    low_left = hop_x(low, 1)
    low_right = hop_x(low, -1)
    high_right = hop_x(high, -1)
    high_left = hop_x(high, 1)
    low_far = hop_x(low_left, 1)
    high_far = hop_x(high_right, -1)
    return [low, high, low_left, high_left, low_right, high_right, low_far, high_far]


def block_source(part):
    dev = lax.axis_index("dev")
    return ((dev >> 2) ^ (part % 4)) * 4 + ((dev + (0, 3, 1, 2)[part // 4]) & 3)


HEIGHTS = (80, 48, 16)
OFFSETS = (0, 80, 128)
PIECE = 144


def early_kernel(out):
    out[...] = jnp.zeros_like(out)


def early():
    return pl.pallas_call(
        early_kernel,
        out_shape=jax.ShapeDtypeStruct((8, 128), F32),
        out_specs=VMEM,
        cost_estimate=pl.CostEstimate(flops=4_000_000_000, bytes_accessed=4096, transcendentals=0),
        compiler_params=pltpu.CompilerParams(vmem_limit_bytes=1 << 20),
        name="early",
    )()


def pack_kernel(owners, slot, unused, *refs):
    outs, held = refs[:4], refs[4]
    group, dev = lax.axis_index("grp"), lax.axis_index("dev")
    row = lax.broadcasted_iota(jnp.int32, (256, 256), 0)
    col = lax.broadcasted_iota(jnp.int32, (256, 256), 1)
    for step in range(3):

        @pl.when(owners[step, group] == dev)
        def _():
            top = 512 * step
            held[top + 256 :] = slot[0, top + 256 :]
            first = slot[0, top : top + 256, :256].astype(F32)
            second = slot[0, top + 256 : top + 512, 256:].astype(F32).T
            held[top + 256 : top + 512, 256:] = jnp.where(row > col, first, second).astype(BF16)
            height = HEIGHTS[step]
            for dx in range(4):
                for bits in range(4):
                    chunk = ((dev >> 2) ^ bits) * 4 + ((dev + dx) & 3)
                    start = pl.multiple_of(top + 256 + chunk * height, 16)
                    outs[dx][bits, :height] = held[pl.ds(start, height)]


def pack(owners, panels, first):
    return pl.pallas_call(
        pack_kernel,
        out_shape=[jax.ShapeDtypeStruct((4, HEIGHTS[0], 512), BF16)] * 4,
        in_specs=[SMEM, VMEM, VMEM],
        out_specs=[VMEM] * 4,
        scratch_shapes=[pltpu.VMEM((1536, 512), BF16)],
        cost_estimate=pl.CostEstimate(flops=1_000_000, bytes_accessed=2_800_000, transcendentals=0),
        compiler_params=pltpu.CompilerParams(vmem_limit_bytes=16 << 20),
        name="pack",
    )(owners, panels, first)


def pick_kernel(owners, *refs):
    chunks, outs = refs[:4], refs[4:]
    group, dev = lax.axis_index("grp"), lax.axis_index("dev")
    for step in range(3):
        first, rows = OFFSETS[step], HEIGHTS[step]
        owner = owners[step, group]
        for dx in range(4):

            @pl.when(owner == (dev >> 2) * 4 + ((dev - dx) & 3))
            def _():
                for bits in range(4):
                    outs[bits][first : first + rows] = chunks[dx][bits, :rows]


def pick(owners, chunks):
    return pl.pallas_call(
        pick_kernel,
        out_shape=[jax.ShapeDtypeStruct((PIECE, 512), BF16)] * 4,
        in_specs=[SMEM] + [VMEM] * 4,
        out_specs=[VMEM] * 4,
        cost_estimate=pl.CostEstimate(flops=1_000_000, bytes_accessed=1_200_000, transcendentals=0),
        compiler_params=pltpu.CompilerParams(vmem_limit_bytes=8 << 20),
        name="pick",
    )(owners, *chunks)


def pick_z_kernel(owners, *refs):
    pieces, out = refs[:4], refs[4]
    group, dev = lax.axis_index("grp"), lax.axis_index("dev")
    for step in range(3):
        first, rows = OFFSETS[step], HEIGHTS[step]
        distance = (owners[step, group] ^ dev) >> 2
        for bits in range(4):

            @pl.when(distance == bits)
            def _():
                out[first : first + rows] = pieces[bits][first : first + rows]


def pick_z(owners, pieces):
    return pl.pallas_call(
        pick_z_kernel,
        out_shape=jax.ShapeDtypeStruct((PIECE, 512), BF16),
        in_specs=[SMEM] + [VMEM] * 4,
        out_specs=VMEM,
        cost_estimate=pl.CostEstimate(flops=1_000_000, bytes_accessed=300_000, transcendentals=0),
        compiler_params=pltpu.CompilerParams(vmem_limit_bytes=4 << 20),
        name="pick_z",
    )(owners, *pieces)


def tile_kernel(*refs):
    panels, strips, (cols, out, pan0, pan1, pan2, border, answer) = refs[:8], refs[8:16], refs[16:]
    half = 256
    pans = (pan0, pan1, pan2)
    sources = [block_source(part) for part in range(16)]
    row = lax.broadcasted_iota(jnp.int32, (half, half), 0)
    col = lax.broadcasted_iota(jnp.int32, (half, half), 1)

    def dot(a, b):
        return jnp.dot(a, b, preferred_element_type=F32)

    def unit(below):
        return jnp.where(row > col, below, jnp.where(row == col, 1.0, 0.0)).astype(BF16)

    def inverse_times(step, current):
        pan, first, rows = pans[step], OFFSETS[step], HEIGHTS[step]
        for part, source in enumerate(sources):
            pan[pl.ds(pl.multiple_of(source * rows, 16), rows)] = panels[part // 2][part % 2, first : first + rows]
        shared = pan[:half, half:].astype(F32)
        high, low = current[:half], current[half:]
        upper = dot(unit(shared), high)
        lower = dot(pan[:half, :half], high) + dot(unit(shared.T), low)
        result = jnp.concatenate([upper, lower], axis=0).astype(BF16)
        answer[step * 512 : step * 512 + 512] = result
        return result

    first = inverse_times(0, cols[:512])
    rest = cols[512:].astype(F32) - dot(pan0[half:], first)
    second = inverse_times(1, rest[:512].astype(BF16))
    rest = rest[512:] - dot(pan1[half:], second)
    inverse_times(2, rest.astype(BF16))
    for part, source in enumerate(sources):
        border[pl.ds(pl.multiple_of(source * 96, 32), 96)] = strips[part // 2][part % 2]
    tile = lax.dot_general(answer[...], border[...], (((0,), (0,)), ((), ())), preferred_element_type=F32)
    for block in range(8):
        out[block] = tile[:, block * 128 : block * 128 + 128].astype(BF16)


def make_tile(panels, strips, cols):
    return pl.pallas_call(
        tile_kernel,
        out_shape=jax.ShapeDtypeStruct((8, 256, 128), BF16),
        in_specs=[VMEM] * 17,
        out_specs=VMEM,
        scratch_shapes=[
            pltpu.VMEM((1280, 512), BF16),
            pltpu.VMEM((768, 512), BF16),
            pltpu.VMEM((256, 512), BF16),
            pltpu.VMEM((1536, 1024), BF16),
            pltpu.VMEM((1536, 256), BF16),
        ],
        cost_estimate=pl.CostEstimate(flops=1_500_000_000, bytes_accessed=8_000_000, transcendentals=0),
        compiler_params=pltpu.CompilerParams(vmem_limit_bytes=32 << 20),
        name="tile",
    )(*panels, *strips, cols)


def place_kernel(block_rows, own, other, *refs):
    outs, total = refs[:8], refs[8]
    group = lax.axis_index("grp")
    core = group & 1
    total[...] = jnp.zeros_like(total)
    for part in range(16):
        source, giver = (own, group) if part < 8 else (other, group ^ 1)
        target = block_rows[part % 8, giver]
        owner = target >> 1
        slot = (((owner >> 2) - (group >> 2)) & 3) * 4 + (((owner ^ group) >> 1) & 1) * 2 + (target & 1)

        @pl.when((owner & 1) == core)
        def _():
            total[slot] += source[part % 8].astype(F32)

    for dy in range(4):
        for half in range(2):
            outs[half * 4 + dy][...] = total[dy * 4 + half * 2 : dy * 4 + half * 2 + 2].astype(BF16)


def place(block_rows, own, other):
    return pl.pallas_call(
        place_kernel,
        out_shape=[jax.ShapeDtypeStruct((2, 256, 128), BF16)] * 8,
        in_specs=[SMEM, VMEM, VMEM],
        out_specs=[VMEM] * 8,
        scratch_shapes=[pltpu.VMEM((16, 256, 128), F32)],
        cost_estimate=pl.CostEstimate(flops=1_000_000, bytes_accessed=2_000_000, transcendentals=0),
        compiler_params=pltpu.CompilerParams(vmem_limit_bytes=32 << 20),
        name="place",
    )(block_rows, own, other)


def add_y(parts):
    moved = [part.astype(F32) for part in [parts[0]] + [hop_y(parts[dy], dy) for dy in (1, 2, 3)]]
    return (moved[0] + moved[2]) + (moved[1] + moved[3])


def step(panels, panel_owner, interface_cols, border, block_rows, pattern, block_x):
    strips = gather_border(border.T)

    chunks = pack(panel_owner.T, panels, early())
    far = hop_x(chunks[2], 2)
    chunks = [chunks[0], hop_x(chunks[1], 1), far, hop_x(chunks[3], 3)]
    pieces = pick(panel_owner.T, chunks)
    pieces = [pieces[0]] + hops_z(pieces[1:])
    piece = pick_z(panel_owner.T, pieces)
    tile = make_tile(gather_panel(piece), strips, interface_cols)

    placed = place(block_rows.T, tile, swap_grp(tile, 1))
    other = add_y(placed[4:])
    mine = add_y(placed[:4])
    other = swap_grp(other.astype(BF16), 2)
    own_rows = (mine + other.astype(F32)).transpose(0, 2, 1)
    masked = own_rows.reshape(2, 128, 2, 128) * pattern.astype(F32)[:, None, :, None]
    schur = masked.reshape(256, 256).astype(BF16)

    partial = jnp.dot(schur, block_x, preferred_element_type=F32).astype(BF16)
    moved = [part.astype(F32) for part in [partial] + hops_z([partial] * 3)]
    line_sum = ((moved[0] + moved[1]) + (moved[2] + moved[3])).astype(BF16)
    moved = [part.astype(F32) for part in [line_sum] + [hop_x(line_sum, dx) for dx in (1, 2, 3)]]
    product = (moved[0] + moved[2]) + (moved[1] + moved[3])
    return (schur, product)


def solution(mesh):
    return jax.shard_map(
        step,
        mesh=mesh,
        in_specs=(
            P(("grp", "dev"), None, None),
            P(),
            P(None, ("grp", "dev")),
            P("grp", "dev"),
            P(),
            P("grp", "dev"),
            P("dev", None),
        ),
        out_specs=(P("grp", "dev"), P("grp", None)),
        check_vma=False,
    )
```
